32 devices in a mesh: row: 4 (over y, x), col: 8 (over z, core).
Axes of the slice: x: 2, y: 2, z: 4, core: 2. Of those that a mesh axis runs over, the one named last changes fastest.
Arguments:
- trail: float32 [2, 4, 512, 2, 8, 512], P(None, 'row', None, None, 'col'), may hold values from -6 to 6
- panel: float32 [2, 4, 512, 512], P(None, 'row', None, 'col'), may hold values from -6 to 6
- row_basis: float32 [2, 4, 64, 512], P(None, 'row', None, 'col'), may hold values from -0.75 to 0.75
- row_coeff: float32 [2, 4, 64, 512], P(None, 'row', None, 'col'), may hold values from -0.25 to 0.25
- col_basis: float32 [2, 8, 64, 512], P(None, 'col', None, 'row'), may hold values from -0.75 to 0.75
- col_scaled: float32 [2, 8, 64, 512], P(None, 'col', None, 'row'), may hold values from -0.25 to 0.25
- pivot_basis: float32 [64, 512], P(None, 'col'), may hold values from -0.75 to 0.75
- pivot_scaled: float32 [64, 512], replicated, may hold values from -0.25 to 0.25
- sketch: float32 [64, 512], replicated, may hold values from -6 to 6
- perm: int32 [512], replicated, may hold values from 0 to 511, each once
- pair_kind: int32 [256], replicated, may hold values from 0 to 1
- pivot_values: float32 [3, 256], replicated, may hold values from -3 to 3, as said below
Outputs:
- trail_out: float32 [2, 4, 512, 2, 8, 512], P(None, 'row', None, None, 'col')
- basis_out: float32 [2, 4, 64, 512], P(None, 'row')
- coeff_out: float32 [2, 4, 64, 512], P(None, 'row')
The draws below stay inside these ranges and needn't reach their ends.
Inputs may be any that keep to these rules, and one draw needn't show every extreme that they name: `pivot_values`: rows 0 and 1 have magnitudes between 0.5 and 0.7; row 2 has magnitude 1.2 or more.
All inputs are finite; a program needn't handle non-finite values.
Results may differ from the reference program's by a relative error of at most 0.00013.
Values sent between devices are 32-bit elements; how exact they have to be, the bound alone decides.
No kernel may reach another device: no remote copies, remote signals or barrier semaphores. Data moves between devices by JAX's collectives and lax.ppermute only.
A program may use at most 64 MiB of HBM per device.

```python
import jax
import jax.numpy as jnp
from jax import lax

B = 512
R = 64
LR = 2
LC = 2
PAIRS = 256
N_ROW = 4
N_COL = 8


def draw_pivot_values(key, part):
    first_key, second_key, third_key = jax.random.split(jax.random.fold_in(key, 17), 3)
    lowest, highest = (1.2, 2.0)
    magnitudes = jax.random.uniform(first_key, (2, PAIRS), jnp.float32, 0.5, 0.7)
    signs = jnp.where(jax.random.bernoulli(second_key, 0.5, (3, PAIRS)), 1.0, -1.0)
    offdiag = jax.random.uniform(third_key, (1, PAIRS), jnp.float32, lowest, highest)
    return jnp.concatenate([magnitudes, offdiag], axis=0) * signs


def place_ends(entries, stream_key, smallest, largest):
    place = [jax.random.randint(jax.random.fold_in(stream_key, axis), (), 0, length) for axis, length in enumerate(entries.shape)]
    main_axis = entries.shape.index(max(entries.shape))
    neighbour = place[:main_axis] + [(place[main_axis] + 1) % entries.shape[main_axis]] + place[main_axis + 1:]
    return entries.at[tuple(place)].set(smallest).at[tuple(neighbour)].set(largest)


def shard_levels(rng, dims, shards, smallest, high):
    loudness, own = 1.0, jax.random.fold_in(rng, 6)
    for position, blocks in shards:
        draws = jnp.exp(jax.random.uniform(jax.random.fold_in(own, position), (blocks,), jnp.float32, smallest / len(shards), high / len(shards)))
        loudness = loudness * jnp.repeat(draws, dims[position] // blocks).reshape([-1 if axis == position else 1 for axis in range(len(dims))])
    return loudness


def scatter_about(stream_key, shape, width, reach, shards=(), dtype=jnp.bfloat16):
    array = width * jax.random.normal(stream_key, shape, jnp.float32)
    if shards:
        array = array * shard_levels(stream_key, shape, shards, -0.22, 0.18)
    return jnp.clip(array, -reach, reach).astype(dtype)


def setup_inputs(seed: int = 0) -> dict:
    keys = jax.random.split(jax.random.key(seed), 13)
    trail = scatter_about(keys[0], (LR, N_ROW, B, LC, N_COL, B), 1.0, 6.0, ((1, 4), (4, 8)), jnp.float32)
    panel = scatter_about(keys[1], (LR, N_ROW, B, B), 1.0, 6.0, ((1, 4), (3, 8)), jnp.float32)
    row_basis = scatter_about(keys[2], (LR, N_ROW, R, B), R ** -0.5, 0.75, ((1, 4), (3, 8)), jnp.float32)
    row_coeff = scatter_about(keys[3], (LR, N_ROW, R, B), B ** -0.5, 0.25, ((1, 4), (3, 8)), jnp.float32)
    col_basis = scatter_about(keys[4], (LC, N_COL, R, B), R ** -0.5, 0.75, ((1, 8), (3, 4)), jnp.float32)
    col_scaled = scatter_about(keys[5], (LC, N_COL, R, B), B ** -0.5, 0.25, ((1, 8), (3, 4)), jnp.float32)
    pivot_basis = scatter_about(keys[6], (R, B), R ** -0.5, 0.75, ((1, 8),), jnp.float32)
    pivot_scaled = scatter_about(keys[7], (R, B), B ** -0.5, 0.25, (), jnp.float32)
    sketch = scatter_about(keys[8], (R, B), 1.0, 6.0, (), jnp.float32)
    perm = jax.random.permutation(keys[9], B).astype(jnp.int32)
    pair_kind = place_ends(jax.random.randint(keys[10], (PAIRS,), 0, 2), jax.random.fold_in(keys[10], 1), 0, 1).astype(jnp.int32)
    pivot_values = draw_pivot_values(jax.random.fold_in(keys[12], 71), 0)
    return {"trail": trail, "panel": panel, "row_basis": row_basis, "row_coeff": row_coeff, "col_basis": col_basis, "col_scaled": col_scaled, "pivot_basis": pivot_basis, "pivot_scaled": pivot_scaled, "sketch": sketch, "perm": perm, "pair_kind": pair_kind, "pivot_values": pivot_values}


def pair_apply(rows, pair_kind, pivot_values):
    shaped = rows.reshape(rows.shape[:-1] + (rows.shape[-1] // 2, 2))
    first_in = shaped[..., 0]
    second_in = shaped[..., 1]
    diag_one = pivot_values[0]
    diag_two = pivot_values[1]
    offdiag = pivot_values[2]
    determinant = diag_one * diag_two - offdiag * offdiag
    twin = pair_kind == 1
    first = jnp.where(twin, (first_in * diag_two - second_in * offdiag) / determinant, first_in / diag_one)
    second = jnp.where(twin, (second_in * diag_one - first_in * offdiag) / determinant, second_in / diag_two)
    return jnp.stack([first, second], axis=-1).reshape(rows.shape)

def reference(trail, panel, row_basis, row_coeff, col_basis, col_scaled, pivot_basis, pivot_scaled, sketch, perm, pair_kind, pivot_values):
    highest = lax.Precision.HIGHEST
    xrows = row_basis.reshape(LR * N_ROW, R, B)
    yrows = row_coeff.reshape(LR * N_ROW, R, B)
    zcols = col_basis.reshape(LC * N_COL, R, B)
    gcols = col_scaled.reshape(LC * N_COL, R, B)
    tiles = trail.reshape(LR * N_ROW, B, LC * N_COL, B)

    def one_row(item):
        tile, xrow, yrow = item
        core = jnp.einsum('rp,jsp->rjs', yrow, gcols, precision=highest)
        left = jnp.einsum('rp,rjs->pjs', xrow, core, precision=highest)
        change = jnp.einsum('pjs,jsq->pjq', left, zcols, precision=highest)
        return tile - change
    trail_out = lax.map(one_row, (tiles, xrows, yrows)).reshape(trail.shape)
    panels = panel.reshape(LR * N_ROW, B, B)
    pcore = jnp.einsum('irp,sp->irs', yrows, pivot_scaled, precision=highest)
    pleft = jnp.einsum('irp,irs->ips', xrows, pcore, precision=highest)
    updated = panels - jnp.einsum('ips,sq->ipq', pleft, pivot_basis, precision=highest)
    scaled_t = pair_apply(sketch, pair_kind, pivot_values)
    permuted = jnp.take(updated, perm, axis=2)
    range_t = jnp.einsum('ipt,rt->irp', permuted, scaled_t, precision=highest)
    gram = jnp.einsum('irp,isp->irs', range_t, range_t, precision=highest) / B
    lower = jnp.linalg.cholesky(gram)
    basis = jax.vmap(lambda low, rhs: jax.scipy.linalg.solve_triangular(low, rhs, lower=True))(lower, range_t)
    projected = jnp.einsum('irp,ipt->irt', basis, permuted, precision=highest)
    coeff = pair_apply(projected, pair_kind, pivot_values) / jnp.sqrt(jnp.float32(B))
    return (trail_out, basis.reshape(LR, N_ROW, R, B), coeff.reshape(LR, N_ROW, R, B))
```

```python
import jax
import jax.numpy as jnp
from jax import lax
from jax.experimental import pallas as pl
from jax.experimental.pallas import tpu as pltpu
from jax.sharding import PartitionSpec as P

F32 = jnp.float32
BF16 = jnp.bfloat16
HIGHEST = lax.Precision.HIGHEST


def dot_nn(left, right):
    return lax.dot_general(
        left, right, (((1,), (0,)), ((), ())), precision=HIGHEST, preferred_element_type=F32
    )


def dot_nt(left, right):
    return lax.dot_general(
        left, right, (((1,), (1,)), ((), ())), precision=HIGHEST, preferred_element_type=F32
    )


def split3(x):
    high = x.astype(BF16)
    rest = x - high.astype(F32)
    mid = rest.astype(BF16)
    low = (rest - mid.astype(F32)).astype(BF16)
    return high, mid, low


def onehot_dot(x, onehot, dims):
    parts = [
        lax.dot_general(part, onehot, (dims, ((), ())), preferred_element_type=F32)
        for part in split3(x)
    ]
    return parts[0] + (parts[1] + parts[2])


def call(kernel, outs, *args, scratch=(), flops=0, name=None):
    vmem = pl.BlockSpec(memory_space=pltpu.VMEM)
    many = isinstance(outs, (list, tuple))
    return pl.pallas_call(
        kernel,
        out_shape=outs,
        in_specs=[vmem] * len(args),
        out_specs=[vmem] * len(outs) if many else vmem,
        scratch_shapes=list(scratch),
        cost_estimate=pl.CostEstimate(flops=flops, transcendentals=0, bytes_accessed=1 << 20),
        name=name,
    )(*args)


def shape(*dims):
    return jax.ShapeDtypeStruct(dims, F32)


def pair_scale(rows, diag, off):
    length = rows.shape[1]
    lane = lax.broadcasted_iota(jnp.int32, rows.shape, 1)
    after = pltpu.roll(rows, length - 1, 1)
    before = pltpu.roll(rows, 1, 1)
    return rows * diag + jnp.where(lane % 2 == 0, after, before) * off


def selector_of(perm):
    length = perm.shape[1]
    row = lax.broadcasted_iota(jnp.int32, (length, length), 0)
    return (row == perm).astype(F32).astype(BF16)


def sketch_kernel(sketch_ref, perm_ref, kind_ref, values_ref, out_ref, coef_ref):
    pairs = kind_ref.shape[1]
    length = perm_ref.shape[1]
    one, two, cross = values_ref[0:1, :], values_ref[1:2, :], values_ref[2:3, :]
    twin = kind_ref[...] == 1
    det = one * two - cross * cross
    first = jnp.where(twin, two / det, 1.0 / one)
    second = jnp.where(twin, one / det, 1.0 / two)
    mixed = jnp.where(twin, -cross / det, 0.0)
    row = lax.broadcasted_iota(jnp.int32, (8, pairs), 0)
    stacked = jnp.where(row == 0, first, jnp.where(row == 1, second, mixed))
    pair = lax.broadcasted_iota(jnp.int32, (pairs, length), 0)
    lane = lax.broadcasted_iota(jnp.int32, (pairs, length), 1)
    even = (lane == 2 * pair).astype(F32).astype(BF16)
    odd = (lane == 2 * pair + 1).astype(F32).astype(BF16)
    at_even = onehot_dot(stacked, even, ((1,), (0,)))
    at_odd = onehot_dot(stacked, odd, ((1,), (0,)))
    diag = at_even[0:1] + at_odd[1:2]
    off = at_even[2:3] + at_odd[2:3]
    coef_ref[0:1, :] = diag
    coef_ref[1:2, :] = off
    scaled = pair_scale(sketch_ref[...], diag, off)
    placed = onehot_dot(scaled, selector_of(perm_ref[...]), ((1,), (1,)))
    chips, _, width = out_ref.shape
    for chip in range(chips):
        out_ref[chip] = placed[:, chip * width : (chip + 1) * width]


def pack_kernel(own_ref, other_ref, factors_ref, others_ref, panel_ref, sent_ref, *piece_refs):
    core = lax.axis_index("col") % 2
    chip = lax.axis_index("col") // 2
    part = own_ref.shape[1]
    width = 2 * part
    mine = factors_ref[...]
    theirs = others_ref[...]
    mine = jnp.where(core == 0, mine[:, :part], mine[:, part:])
    theirs = jnp.where(core == 0, theirs[:, :part], theirs[:, part:])
    sent_ref[:, :part] = jnp.where(core == 0, mine, theirs)
    sent_ref[:, part:] = jnp.where(core == 0, theirs, mine)
    panel_ref[pl.ds(pl.multiple_of(core * part, part), part), :] = own_ref[core]
    panel_ref[pl.ds(pl.multiple_of((1 - core) * part, part), part), :] = other_ref[core]
    chips = len(piece_refs)
    for step in range(chips):
        for target in range(chips):

            @pl.when((chip ^ step) == target)
            def _(step=step, target=target):
                piece_refs[step][...] = panel_ref[:, target * width : (target + 1) * width]


def range_kernel(sketch_ref, *refs):
    piece_refs, out_ref = refs[:-1], refs[-1]
    chip = lax.axis_index("col") // 2
    total = dot_nn(sketch_ref[chip], piece_refs[0][...])
    for step in range(1, len(piece_refs)):
        total = total + dot_nn(sketch_ref[chip ^ step], piece_refs[step][...])
    out_ref[...] = total


def stack_kernel(*refs):
    piece_refs, out_ref = refs[:-1], refs[-1]
    chip = lax.axis_index("col") // 2
    for step, piece_ref in enumerate(piece_refs):
        out_ref[chip ^ step] = piece_ref[...]


def lanes(ref, low, high):
    return jnp.concatenate([ref[chip, low:high, :] for chip in range(ref.shape[0])], axis=1)


def correction_kernel(own_ref, other_ref, pivot_ref, sketch_ref, corr_ref, pcore_ref, pbasis_ref):
    core = lax.axis_index("col") % 2
    chip = lax.axis_index("col") // 2
    rank = pivot_ref.shape[0]
    half = rank // 2
    xrow = lanes(own_ref, 0, rank)
    yrow = lanes(own_ref, rank, 2 * rank)
    mine = lanes(own_ref, 2 * rank, 2 * rank + half)
    theirs = lanes(other_ref, 2 * rank, 2 * rank + half)
    pbasis = jnp.concatenate(
        [jnp.where(core == 0, mine, theirs), jnp.where(core == 0, theirs, mine)], axis=0
    )
    pcore = dot_nt(yrow, pivot_ref[...])
    sketched = dot_nt(lanes(sketch_ref, 0, rank), pbasis)
    mixed = dot_nt(sketched, pcore)
    corr_ref[...] = dot_nn(mixed, xrow)
    pcore_ref[...] = pcore
    mine = own_ref[chip, 2 * rank : 2 * rank + half, :]
    theirs = other_ref[chip, 2 * rank : 2 * rank + half, :]
    pbasis_ref[:half, :] = jnp.where(core == 0, mine, theirs)
    pbasis_ref[half:, :] = jnp.where(core == 0, theirs, mine)


def gram_kernel(corr_ref, pcore_ref, pbasis_ref, panel_ref, own_ref, *refs):
    piece_refs, (range_ref, gram_ref, proj_ref, stack_ref) = refs[:-4], refs[-4:]
    chip = lax.axis_index("col") // 2
    rank = pcore_ref.shape[0]
    for step, piece_ref in enumerate(piece_refs):
        stack_ref[chip ^ step] = piece_ref[...]
    ranges = lanes(stack_ref, 0, rank) - corr_ref[...]
    range_ref[...] = ranges
    gram_ref[...] = dot_nt(ranges, ranges) / ranges.shape[1]
    crossed = dot_nt(ranges, lanes(own_ref, 0, rank))
    proj_ref[...] = dot_nt(ranges, panel_ref[...]) - dot_nn(
        dot_nn(crossed, pcore_ref[...]), pbasis_ref[...]
    )


def factor_kernel(gram_ref, range_ref, inverse_ref, basis_ref):
    rank = gram_ref.shape[0]
    row = lax.broadcasted_iota(jnp.int32, (rank, rank), 0)
    col = lax.broadcasted_iota(jnp.int32, (rank, rank), 1)
    work = jnp.concatenate([gram_ref[...], (row == col).astype(F32)], axis=1)
    rows = lax.broadcasted_iota(jnp.int32, (rank, 2 * rank), 0)
    scale = jnp.ones((rank, 1), F32)
    index = lax.broadcasted_iota(jnp.int32, (rank, 1), 0)
    for step in range(rank):
        pivot_row = work[step : step + 1, :]
        pivot = pivot_row[:, step : step + 1]
        ratio = work[:, step : step + 1] / pivot
        scale = jnp.where(index == step, lax.rsqrt(pivot), scale)
        work = jnp.where(rows > step, work - ratio * pivot_row, work)
    inverse = work[:, rank:] * scale
    inverse_ref[...] = inverse
    basis_ref[...] = dot_nn(inverse, range_ref[...])


def coeff_kernel(inverse_ref, perm_ref, coef_ref, *refs):
    piece_refs, (out_ref, stack_ref) = refs[:-2], refs[-2:]
    chip = lax.axis_index("col") // 2
    rank = inverse_ref.shape[0]
    for step, piece_ref in enumerate(piece_refs):
        stack_ref[chip ^ step] = piece_ref[...]
    projected = dot_nn(inverse_ref[...], lanes(stack_ref, 0, rank))
    permuted = onehot_dot(projected, selector_of(perm_ref[...]), ((1,), (0,)))
    length = permuted.shape[1]
    out_ref[...] = pair_scale(permuted, coef_ref[0:1, :], coef_ref[1:2, :]) / jnp.sqrt(
        jnp.float32(length)
    )


def join_kernel(own_ref, other_ref, out_ref):
    core = lax.axis_index("col") % 2
    out_ref[core] = own_ref[...]
    out_ref[1 - core] = other_ref[...]


def trail_kernel(
    trail_ref, own_ref, other_ref, cols_ref, out_ref, left_ref, right_ref
):
    tile = pl.program_id(0)
    block = pl.program_id(1)
    core = lax.axis_index("col") % 2
    row = lax.axis_index("row")
    ncols, _, deep = left_ref.shape[1], left_ref.shape[2], left_ref.shape[3]
    rank = deep // 3
    nrow = cols_ref.shape[0]
    groups = right_ref.shape[2] // 128
    rows = trail_ref.shape[1] // (ncols * groups)

    @pl.when((tile == 0) & (block == 0))
    def _():
        def whole(col, low):
            base = col * 2 * rank + low * rank
            return jnp.concatenate(
                [cols_ref[part, base : base + rank, :] for part in range(nrow)], axis=1
            )

        for col in range(ncols):
            basis = whole(col, 0)
            scaled = whole(col, 1)
            high = basis.astype(BF16)
            low = (basis - high.astype(F32)).astype(BF16)
            right_ref[col, :rank, :] = high
            right_ref[col, rank : 2 * rank, :] = high
            right_ref[col, 2 * rank :, :] = low
            for index in range(2):
                source = own_ref if index == 0 else other_ref
                xrow = lanes(source, 0, rank)
                yrow = lanes(source, rank, 2 * rank)
                left = dot_nn(dot_nt(scaled, yrow), xrow).T
                high = left.astype(BF16)
                low = (left - high.astype(F32)).astype(BF16)
                where = core if index == 0 else 1 - core
                left_ref[where, col, :, :rank] = high
                left_ref[where, col, :, rank : 2 * rank] = low
                left_ref[where, col, :, 2 * rank :] = high

    start = pl.multiple_of(block * rows, rows)
    for col in range(ncols):
        change = jnp.dot(
            left_ref[tile, col, pl.ds(start, rows), :],
            right_ref[col],
            preferred_element_type=F32,
        )
        for group in range(groups):
            where = pl.ds(col * groups + group, rows, stride=ncols * groups)
            out_ref[0, where, :] = (
                trail_ref[0, where, :] - change[:, group * 128 : (group + 1) * 128]
            )


def trail_call(trail, own, other, cols):
    tiles, _, size, ncols, _, width = trail.shape
    rank = cols.shape[1] // (2 * ncols)
    groups = width // 128
    rows = 128
    view = trail.reshape(tiles, size * ncols * groups, 128)
    block = pl.BlockSpec((1, rows * ncols * groups, 128), lambda a, p: (a, p, 0))
    vmem = pl.BlockSpec(memory_space=pltpu.VMEM)
    out = pl.pallas_call(
        trail_kernel,
        out_shape=jax.ShapeDtypeStruct(view.shape, F32),
        grid=(tiles, size // rows),
        in_specs=[block, vmem, vmem, vmem],
        out_specs=block,
        scratch_shapes=[
            pltpu.VMEM((tiles, ncols, size, 3 * rank), BF16),
            pltpu.VMEM((ncols, 3 * rank, width), BF16),
        ],
        cost_estimate=pl.CostEstimate(
            flops=6 * tiles * ncols * size * rank * width,
            transcendentals=0,
            bytes_accessed=2 * view.size * 4,
        ),
        name="trail",
    )(view, own, other, cols)
    return out.reshape(trail.shape)


def body_of(nrow, ncol):
    chips = ncol // 2
    partner = [(i, i ^ 1) for i in range(ncol)]

    def swap(x):
        return lax.ppermute(x, "col", partner)

    def exchange(pieces):
        return [pieces[0]] + [
            lax.ppermute(pieces[s], "col", [(i, i ^ (2 * s)) for i in range(ncol)])
            for s in range(1, chips)
        ]

    def body(
        trail,
        panel,
        row_basis,
        row_coeff,
        col_basis,
        col_scaled,
        pivot_basis,
        pivot_scaled,
        sketch,
        perm,
        pair_kind,
        pivot_values,
    ):
        tiles, _, size, part = panel.shape
        rank = sketch.shape[0]
        half = rank // 2
        width = 2 * part
        panel_t = jnp.transpose(panel[:, 0], (0, 2, 1))
        perm_row = perm.reshape(1, -1)
        panel_other = swap(panel_t)
        factors = jnp.concatenate(
            [
                jnp.concatenate([row_basis[0, 0], row_basis[1, 0]], axis=1),
                jnp.concatenate([row_coeff[0, 0], row_coeff[1, 0]], axis=1),
                jnp.concatenate([pivot_basis[:half], pivot_basis[half:]], axis=1),
            ],
            axis=0,
        )
        factors_other = swap(factors)
        cols = jnp.concatenate(
            [x[b, 0] for b in range(col_basis.shape[0]) for x in (col_basis, col_scaled)], axis=0
        )
        cols_parts = [cols] + [
            lax.ppermute(cols, "row", [(i, i ^ s) for i in range(nrow)]) for s in range(1, nrow)
        ]
        sketch_t, coef = call(
            sketch_kernel,
            [shape(chips, rank, width), shape(2, size)],
            sketch,
            perm_row,
            pair_kind.reshape(1, -1),
            pivot_values,
            flops=1 << 28,
            name="sketch",
        )
        panel_mine, sent, *pieces = call(
            pack_kernel,
            [shape(width, size), shape(factors.shape[0], width)] + [shape(width, width)] * chips,
            panel_t,
            panel_other,
            factors,
            factors_other,
            name="pack",
        )
        pieces = exchange(pieces)
        sent = exchange([sent] * chips)
        partial = call(range_kernel, shape(rank, width), sketch_t, *pieces, flops=1 << 26, name="range")
        partials = exchange([partial] * chips)
        own = call(stack_kernel, shape(chips, factors.shape[0], width), *sent, name="stack")
        other = swap(own)
        corr, pcore, pbasis = call(
            correction_kernel,
            [shape(rank, size), shape(rank, rank), shape(rank, width)],
            own,
            other,
            pivot_scaled,
            sketch_t,
            flops=1 << 26,
            name="correction",
        )

        def stack_rows(*refs):
            piece_refs, out_ref = refs[:-1], refs[-1]
            row = lax.axis_index("row")
            for step, piece_ref in enumerate(piece_refs):
                out_ref[row ^ step] = piece_ref[...]

        cols_all = call(stack_rows, shape(nrow, *cols.shape), *cols_parts, name="cols")
        trail_out = trail_call(trail, own, other, cols_all)
        ranges, gram, proj = call(
            gram_kernel,
            [shape(rank, size), shape(rank, rank), shape(rank, width)],
            corr,
            pcore,
            pbasis,
            panel_mine,
            own,
            *partials,
            scratch=[pltpu.VMEM((chips, rank, width), F32)],
            flops=1 << 26,
            name="gram",
        )
        projs = exchange([proj] * chips)
        inverse, basis = call(
            factor_kernel, [shape(rank, rank), shape(rank, size)], gram, ranges, flops=1 << 28, name="factor"
        )
        basis_other = swap(basis)
        coeff = call(
            coeff_kernel,
            shape(rank, size),
            inverse,
            perm_row,
            coef,
            *projs,
            scratch=[pltpu.VMEM((chips, rank, width), F32)],
            flops=1 << 28,
            name="coeff",
        )
        coeff_other = swap(coeff)
        basis_out = call(join_kernel, shape(2, rank, size), basis, basis_other, name="join")
        coeff_out = call(join_kernel, shape(2, rank, size), coeff, coeff_other, name="join")
        return (trail_out, basis_out[:, None], coeff_out[:, None])

    return body


def solution(mesh):
    return jax.shard_map(
        body_of(mesh.shape["row"], mesh.shape["col"]),
        mesh=mesh,
        in_specs=(
            P(None, "row", None, None, "col", None),
            P(None, "row", None, "col"),
            P(None, "row", None, "col"),
            P(None, "row", None, "col"),
            P(None, "col", None, "row"),
            P(None, "col", None, "row"),
            P(None, "col"),
            P(),
            P(),
            P(),
            P(),
            P(),
        ),
        out_specs=(
            P(None, "row", None, None, "col", None),
            P(None, "row", None, None),
            P(None, "row", None, None),
        ),
        check_vma=False,
    )
```

```python
import jax
import jax.numpy as jnp
from jax import lax
from jax.experimental import pallas as pl
from jax.experimental.pallas import tpu as pltpu
from jax.sharding import PartitionSpec as P

F32 = jnp.float32
BF16 = jnp.bfloat16
HIGHEST = lax.Precision.HIGHEST


def dot_nn(left, right):
    return lax.dot_general(
        left, right, (((1,), (0,)), ((), ())), precision=HIGHEST, preferred_element_type=F32
    )


def dot_nt(left, right):
    return lax.dot_general(
        left, right, (((1,), (1,)), ((), ())), precision=HIGHEST, preferred_element_type=F32
    )


def split3(x):
    high = x.astype(BF16)
    rest = x - high.astype(F32)
    mid = rest.astype(BF16)
    low = (rest - mid.astype(F32)).astype(BF16)
    return high, mid, low


def onehot_dot(x, onehot, dims):
    parts = [
        lax.dot_general(part, onehot, (dims, ((), ())), preferred_element_type=F32)
        for part in split3(x)
    ]
    return parts[0] + (parts[1] + parts[2])


def call(kernel, outs, *args, scratch=(), flops=0, name=None):
    vmem = pl.BlockSpec(memory_space=pltpu.VMEM)
    many = isinstance(outs, (list, tuple))
    return pl.pallas_call(
        kernel,
        out_shape=outs,
        in_specs=[vmem] * len(args),
        out_specs=[vmem] * len(outs) if many else vmem,
        scratch_shapes=list(scratch),
        cost_estimate=pl.CostEstimate(flops=flops, transcendentals=0, bytes_accessed=1 << 20),
        compiler_params=pltpu.CompilerParams(vmem_limit_bytes=8 << 20),
        name=name,
    )(*args)


def shape(*dims):
    return jax.ShapeDtypeStruct(dims, F32)


def pair_scale(rows, diag, off):
    length = rows.shape[1]
    lane = lax.broadcasted_iota(jnp.int32, rows.shape, 1)
    after = pltpu.roll(rows, length - 1, 1)
    before = pltpu.roll(rows, 1, 1)
    return rows * diag + jnp.where(lane % 2 == 0, after, before) * off


def selector_of(perm):
    length = perm.shape[1]
    row = lax.broadcasted_iota(jnp.int32, (length, length), 0)
    return (row == perm).astype(F32).astype(BF16)


def sketch_kernel(sketch_ref, perm_ref, kind_ref, values_ref, out_ref, coef_ref):
    pairs = kind_ref.shape[1]
    length = perm_ref.shape[1]
    one, two, cross = values_ref[0:1, :], values_ref[1:2, :], values_ref[2:3, :]
    twin = kind_ref[...] == 1
    det = one * two - cross * cross
    first = jnp.where(twin, two / det, 1.0 / one)
    second = jnp.where(twin, one / det, 1.0 / two)
    mixed = jnp.where(twin, -cross / det, 0.0)
    row = lax.broadcasted_iota(jnp.int32, (8, pairs), 0)
    stacked = jnp.where(row == 0, first, jnp.where(row == 1, second, mixed))
    pair = lax.broadcasted_iota(jnp.int32, (pairs, length), 0)
    lane = lax.broadcasted_iota(jnp.int32, (pairs, length), 1)
    even = (lane == 2 * pair).astype(F32).astype(BF16)
    odd = (lane == 2 * pair + 1).astype(F32).astype(BF16)
    at_even = onehot_dot(stacked, even, ((1,), (0,)))
    at_odd = onehot_dot(stacked, odd, ((1,), (0,)))
    diag = at_even[0:1] + at_odd[1:2]
    off = at_even[2:3] + at_odd[2:3]
    coef_ref[0:1, :] = diag
    coef_ref[1:2, :] = off
    scaled = pair_scale(sketch_ref[...], diag, off)
    placed = onehot_dot(scaled, selector_of(perm_ref[...]), ((1,), (1,)))
    chips, _, width = out_ref.shape
    for chip in range(chips):
        out_ref[chip] = placed[:, chip * width : (chip + 1) * width]


def stages(size):
    bits = []
    bit = size // 2
    while bit:
        bits.append(bit)
        bit //= 2
    return bits


def codes(size):
    order = [0]
    for bit in stages(size):
        order = order + [code ^ bit for code in order]
    return order


def stack_kernel(*refs):
    piece_refs, out_ref = refs[:-1], refs[-1]
    at = 0
    for piece_ref in piece_refs:
        out_ref[at : at + piece_ref.shape[0]] = piece_ref[...]
        at += piece_ref.shape[0]


def stack(*pieces):
    total = sum(piece.shape[0] for piece in pieces)
    return call(stack_kernel, shape(total, *pieces[0].shape[1:]), *pieces, name="stack")


def gather(x, size, send):
    pieces = [x]
    for bit in stages(size):
        held = pieces[0] if len(pieces) == 1 else stack(*pieces)
        pieces = [held, send(held, bit)]
    return pieces


def entries(refs, size):
    order = codes(size)
    at = 0
    for ref in refs:
        for t in range(ref.shape[0]):
            yield order[at], ref, t
            at += 1


def lanes(ref, *index):
    low, high = index[-2:]
    lead = index[:-2]
    return jnp.concatenate(
        [ref[(chip, *lead, slice(low, high))] for chip in range(ref.shape[0])], axis=1
    )


def factors_kernel(row_basis_ref, row_coeff_ref, pivot_ref, out_ref):
    rank = row_basis_ref.shape[1]
    half = rank // 2
    part = row_basis_ref.shape[2]
    for tile in range(2):
        where = slice(tile * part, (tile + 1) * part)
        out_ref[0, :rank, where] = row_basis_ref[tile]
        out_ref[0, rank : 2 * rank, where] = row_coeff_ref[tile]
        out_ref[0, 2 * rank :, where] = pivot_ref[tile * half : (tile + 1) * half]


def columns_kernel(col_basis_ref, col_scaled_ref, out_ref):
    rank = col_basis_ref.shape[1]
    for col in range(col_basis_ref.shape[0]):
        base = 2 * col * rank
        out_ref[0, base : base + rank] = col_basis_ref[col]
        out_ref[0, base + rank : base + 2 * rank] = col_scaled_ref[col]


def partial_kernel(sketch_ref, own_ref, other_ref, out_ref, panel_ref):
    core = lax.axis_index("col") % 2
    chip = lax.axis_index("col") // 2
    part = own_ref.shape[1]
    panel_ref[pl.ds(pl.multiple_of(core * part, part), part), :] = own_ref[core]
    panel_ref[pl.ds(pl.multiple_of((1 - core) * part, part), part), :] = other_ref[core]
    out_ref[...] = dot_nn(sketch_ref[chip], panel_ref[...])


def add_kernel(left_ref, right_ref, out_ref):
    out_ref[...] = left_ref[...] + right_ref[...]


def prepare_kernel(chips, *refs):
    count = (len(refs) - 6) // 2
    own_refs, other_refs = refs[:count], refs[count : 2 * count]
    pivot_ref, sketch_ref, panel_ref, factors_ref, corr_ref, updated_ref = refs[2 * count :]
    core = lax.axis_index("col") % 2
    chip = lax.axis_index("col") // 2
    rank = pivot_ref.shape[0]
    part = own_refs[0].shape[2] // 2
    for (code, own_ref, t), (_, other_ref, u) in zip(
        entries(own_refs, chips), entries(other_refs, chips)
    ):
        mine, theirs = own_ref[t], other_ref[u]
        for tile in range(2):
            where = slice(tile * part, (tile + 1) * part)
            left = jnp.where(core == 0, mine[:, where], theirs[:, where])
            right = jnp.where(core == 0, theirs[:, where], mine[:, where])
            factors_ref[chip ^ code, tile] = jnp.concatenate([left, right], axis=1)
    xrow = lanes(factors_ref, core, 0, rank)
    yrow = lanes(factors_ref, core, rank, 2 * rank)
    pbasis = jnp.concatenate(
        [lanes(factors_ref, tile, 2 * rank, 2 * rank + rank // 2) for tile in range(2)], axis=0
    )
    pcore = dot_nt(yrow, pivot_ref[...])
    lifted = dot_nn(pcore, pbasis)
    sketched = lanes(sketch_ref, 0, rank)
    corr_ref[...] = dot_nn(dot_nt(sketched, lifted), xrow)
    local = jnp.concatenate(
        [factors_ref[chip, tile, 2 * rank : 2 * rank + rank // 2, :] for tile in range(2)], axis=0
    )
    lifted = dot_nn(pcore, local)
    updated_ref[...] = panel_ref[...] - dot_nn(lifted.T, xrow)


def gram_kernel(left_ref, right_ref, corr_ref, updated_ref, range_ref, gram_ref, proj_ref):
    ranges = (left_ref[...] + right_ref[...]) - corr_ref[...]
    range_ref[...] = ranges
    proj_ref[0] = dot_nt(ranges, updated_ref[...])
    gram_ref[...] = dot_nt(ranges, ranges) / ranges.shape[1]


def factor_kernel(gram_ref, range_ref, out_ref):
    rank = gram_ref.shape[0]
    group = 8
    row = lax.broadcasted_iota(jnp.int32, (group, rank), 0)
    col = lax.broadcasted_iota(jnp.int32, (group, rank), 1)
    work = [
        jnp.concatenate(
            [gram_ref[base : base + group], (row + base == col).astype(F32)], axis=1
        )
        for base in range(0, rank, group)
    ]
    rows = lax.broadcasted_iota(jnp.int32, (group, 2 * rank), 0)
    index = lax.broadcasted_iota(jnp.int32, (group, 1), 0)
    pivots = [jnp.ones((group, 1), F32) for _ in work]
    for step in range(rank):
        at, inner = divmod(step, group)
        pivot_row = work[at][inner : inner + 1]
        pivot = pivot_row[:, step : step + 1]
        pivots[at] = jnp.where(index == inner, pivot, pivots[at])
        scaled = pivot_row / pivot
        for block in range(at, len(work)):
            after = work[block] - work[block][:, step : step + 1] * scaled
            work[block] = jnp.where(rows > inner, after, work[block]) if block == at else after
    inverse = jnp.concatenate(
        [block[:, rank:] * lax.rsqrt(pivot) for block, pivot in zip(work, pivots)], axis=0
    )
    size = range_ref.shape[1]
    out_ref[:, :size] = dot_nn(inverse, range_ref[...])
    out_ref[:, size : size + rank] = inverse


def coeff_kernel(chips, own_ref, other_ref, perm_ref, coef_ref, *refs):
    count = (len(refs) - 3) // 2
    own_refs, other_refs = refs[:count], refs[count : 2 * count]
    basis_ref, coeff_ref, stack_ref = refs[2 * count :]
    core = lax.axis_index("col") % 2
    chip = lax.axis_index("col") // 2
    rank = own_ref.shape[0]
    size = perm_ref.shape[1]
    projected = []
    for source, pieces in ((own_ref, own_refs), (other_ref, other_refs)):
        for code, ref, t in entries(pieces, chips):
            stack_ref[chip ^ code] = ref[t]
        projected.append(dot_nn(source[:, size : size + rank], lanes(stack_ref, 0, rank)))
    both = jnp.concatenate(projected, axis=0)
    permuted = onehot_dot(both, selector_of(perm_ref[...]), ((1,), (0,)))
    result = pair_scale(permuted, coef_ref[0:1, :], coef_ref[1:2, :]) / jnp.sqrt(jnp.float32(size))
    basis_ref[core] = own_ref[:, :size]
    basis_ref[1 - core] = other_ref[:, :size]
    coeff_ref[core] = result[:rank]
    coeff_ref[1 - core] = result[rank:]


def trail_kernel(nrow, trail_ref, factors_ref, *refs):
    col_refs, (out_ref, left_ref, right_ref, cols_ref) = refs[:-4], refs[-4:]
    tile = pl.program_id(0)
    row = lax.axis_index("row")
    ncols, deep, width = right_ref.shape
    rank = deep // 3
    size = left_ref.shape[1]
    groups = width // 128

    @pl.when(tile == 0)
    def _():
        for code, ref, t in entries(col_refs, nrow):
            cols_ref[row ^ code] = ref[t]
        for col in range(ncols):
            basis = lanes(cols_ref, 2 * col * rank, (2 * col + 1) * rank)
            high = basis.astype(BF16)
            right_ref[col, :rank, :] = high
            right_ref[col, rank : 2 * rank, :] = high
            right_ref[col, 2 * rank :, :] = (basis - high.astype(F32)).astype(BF16)

    xrow = lanes(factors_ref, tile, 0, rank)
    yrow = lanes(factors_ref, tile, rank, 2 * rank)
    for col in range(ncols):
        scaled = lanes(cols_ref, (2 * col + 1) * rank, (2 * col + 2) * rank)
        left = dot_nn(dot_nt(scaled, yrow), xrow).T
        high = left.astype(BF16)
        left_ref[col, :, :rank] = high
        left_ref[col, :, rank : 2 * rank] = (left - high.astype(F32)).astype(BF16)
        left_ref[col, :, 2 * rank :] = high
    for col in range(ncols):
        change = jnp.dot(left_ref[col], right_ref[col], preferred_element_type=F32)
        for group in range(groups):
            where = pl.ds(col * groups + group, size, stride=ncols * groups)
            out_ref[0, where, :] = (
                trail_ref[0, where, :] - change[:, group * 128 : (group + 1) * 128]
            )


def trail_call(nrow, trail, factors, cols):
    tiles, _, size, ncols, _, width = trail.shape
    rank = cols[0].shape[1] // (2 * ncols)
    groups = width // 128
    view = trail.reshape(tiles, size * ncols * groups, 128)
    block = pl.BlockSpec((1, size * ncols * groups, 128), lambda a: (a, 0, 0))
    vmem = pl.BlockSpec(memory_space=pltpu.VMEM)
    out = pl.pallas_call(
        lambda *refs: trail_kernel(nrow, *refs),
        out_shape=jax.ShapeDtypeStruct(view.shape, F32),
        grid=(tiles,),
        in_specs=[block] + [vmem] * (1 + len(cols)),
        out_specs=block,
        scratch_shapes=[
            pltpu.VMEM((ncols, size, 3 * rank), BF16),
            pltpu.VMEM((ncols, 3 * rank, width), BF16),
            pltpu.VMEM((nrow, *cols[0].shape[1:]), F32),
        ],
        cost_estimate=pl.CostEstimate(
            flops=6 * tiles * ncols * size * rank * width,
            transcendentals=0,
            bytes_accessed=2 * view.size * 4,
        ),
        compiler_params=pltpu.CompilerParams(vmem_limit_bytes=20 << 20),
        name="trail",
    )(view, factors, *cols)
    return out.reshape(trail.shape)


def body_of(nrow, ncol):
    chips = ncol // 2
    assert chips & (chips - 1) == 0 and nrow & (nrow - 1) == 0

    def to_core(x):
        return lax.ppermute(x, "col", [(i, i ^ 1) for i in range(ncol)])

    def to_chip(x, bit):
        return lax.ppermute(x, "col", [(i, i ^ (2 * bit)) for i in range(ncol)])

    def to_row(x, bit):
        return lax.ppermute(x, "row", [(i, i ^ bit) for i in range(nrow)])

    def body(
        trail,
        panel,
        row_basis,
        row_coeff,
        col_basis,
        col_scaled,
        pivot_basis,
        pivot_scaled,
        sketch,
        perm,
        pair_kind,
        pivot_values,
    ):
        _, _, size, part = panel.shape
        rank = sketch.shape[0]
        half = rank // 2
        width = 2 * part
        panel_t = jnp.transpose(panel[:, 0], (0, 2, 1))
        perm_row = perm.reshape(1, -1)
        panel_other = to_core(panel_t)
        factors = call(
            factors_kernel,
            shape(1, 2 * rank + half, width),
            row_basis[:, 0],
            row_coeff[:, 0],
            pivot_basis,
            name="factors",
        )
        own = gather(factors, chips, to_chip)
        sketch_t, coef = call(
            sketch_kernel,
            [shape(chips, rank, width), shape(2, size)],
            sketch,
            perm_row,
            pair_kind.reshape(1, -1),
            pivot_values,
            flops=1 << 28,
            name="sketch",
        )
        total, panel_mine = call(
            partial_kernel,
            [shape(rank, size), shape(width, size)],
            sketch_t,
            panel_t,
            panel_other,
            flops=1 << 26,
            name="partial",
        )
        bits = stages(chips)[::-1]
        for bit in bits[:-1]:
            total = call(add_kernel, shape(rank, size), total, to_chip(total, bit), name="add")
        remote = to_chip(total, bits[-1])
        cols = gather(
            call(
                columns_kernel,
                shape(1, 2 * rank * col_basis.shape[0], col_basis.shape[3]),
                col_basis[:, 0],
                col_scaled[:, 0],
                name="columns",
            ),
            nrow,
            to_row,
        )
        other = [to_core(piece) for piece in own]
        factors_all, corr, updated = call(
            lambda *refs: prepare_kernel(chips, *refs),
            [shape(chips, 2, 2 * rank + half, width), shape(rank, size), shape(width, size)],
            *own,
            *other,
            pivot_scaled,
            sketch_t,
            panel_mine,
            flops=1 << 26,
            name="prepare",
        )
        ranges, gram, proj = call(
            gram_kernel,
            [shape(rank, size), shape(rank, rank), shape(1, rank, width)],
            total,
            remote,
            corr,
            updated,
            flops=1 << 26,
            name="gram",
        )
        projs = gather(proj, chips, to_chip)
        basis = call(
            factor_kernel, shape(rank, size + 128), gram, ranges, flops=1 << 28, name="factor"
        )
        basis_other = to_core(basis)
        trail_out = trail_call(nrow, trail, factors_all, cols)
        projs_other = [to_core(piece) for piece in projs]
        basis_out, coeff_out = call(
            lambda *refs: coeff_kernel(chips, *refs),
            [shape(2, rank, size)] * 2,
            basis,
            basis_other,
            perm_row,
            coef,
            *projs,
            *projs_other,
            scratch=[pltpu.VMEM((chips, rank, width), F32)],
            flops=1 << 28,
            name="coeff",
        )
        return (trail_out, basis_out[:, None], coeff_out[:, None])

    return body


def solution(mesh):
    return jax.shard_map(
        body_of(mesh.shape["row"], mesh.shape["col"]),
        mesh=mesh,
        in_specs=(
            P(None, "row", None, None, "col", None),
            P(None, "row", None, "col"),
            P(None, "row", None, "col"),
            P(None, "row", None, "col"),
            P(None, "col", None, "row"),
            P(None, "col", None, "row"),
            P(None, "col"),
            P(),
            P(),
            P(),
            P(),
            P(),
        ),
        out_specs=(
            P(None, "row", None, None, "col", None),
            P(None, "row", None, None),
            P(None, "row", None, None),
        ),
        check_vma=False,
    )
```

```python
import jax
import jax.numpy as jnp
from jax import lax
from jax.experimental import pallas as pl
from jax.experimental.pallas import tpu as pltpu
from jax.sharding import PartitionSpec as P


F32 = jnp.float32
BF16 = jnp.bfloat16
HIGHEST = lax.Precision.HIGHEST


def dot_nn(left, right):
    return lax.dot_general(
        left, right, (((1,), (0,)), ((), ())), precision=HIGHEST, preferred_element_type=F32
    )


def dot_nt(left, right):
    return lax.dot_general(
        left, right, (((1,), (1,)), ((), ())), precision=HIGHEST, preferred_element_type=F32
    )


def split3(x):
    high = x.astype(BF16)
    rest = x - high.astype(F32)
    mid = rest.astype(BF16)
    low = (rest - mid.astype(F32)).astype(BF16)
    return high, mid, low


def onehot_dot(x, onehot, dims):
    rows = x.shape[0]
    parts = lax.dot_general(
        jnp.concatenate(split3(x), axis=0),
        onehot,
        (dims, ((), ())),
        preferred_element_type=F32,
    )
    return parts[:rows] + (parts[rows : 2 * rows] + parts[2 * rows :])


def call(kernel, outs, *args, fetched=0, kept=0, scratch=(), flops=0):
    vmem = pl.BlockSpec(memory_space=pltpu.VMEM)
    hbm = pl.BlockSpec(memory_space=pltpu.HBM)
    many = isinstance(outs, (list, tuple))
    args = [
        pltpu.with_memory_space_constraint(x, pltpu.HBM) if n < fetched + kept else x
        for n, x in enumerate(args)
    ]
    buffers = [pltpu.VMEM(x.shape, x.dtype) for x in args[:fetched]]

    def wrapped(*refs):
        refs = list(refs)
        extra = refs[len(refs) - fetched - 1 :] if fetched else []
        if fetched:
            refs = refs[: len(refs) - fetched - 1]
            copies = [
                pltpu.make_async_copy(refs[n], extra[n], extra[-1].at[n]) for n in range(fetched)
            ]
            for copy in copies:
                copy.start()
            for copy in copies:
                copy.wait()
            refs[:fetched] = extra[:fetched]
        kernel(*refs)

    scratch = list(scratch)
    if fetched:
        scratch += buffers + [pltpu.SemaphoreType.DMA((fetched,))]
    return pl.pallas_call(
        wrapped,
        out_shape=outs,
        in_specs=[hbm] * (fetched + kept) + [vmem] * (len(args) - fetched - kept),
        out_specs=[vmem] * len(outs) if many else vmem,
        scratch_shapes=scratch,
        cost_estimate=pl.CostEstimate(flops=flops, transcendentals=0, bytes_accessed=1 << 20),
        compiler_params=pltpu.CompilerParams(vmem_limit_bytes=8 << 20),
    )(*args)


def shape(*dims):
    return jax.ShapeDtypeStruct(dims, F32)


def pair_scale(rows, diag, off):
    length = rows.shape[1]
    lane = lax.broadcasted_iota(jnp.int32, rows.shape, 1)
    after = pltpu.roll(rows, length - 1, 1)
    before = pltpu.roll(rows, 1, 1)
    return rows * diag + jnp.where(lane % 2 == 0, after, before) * off


def selector_of(perm):
    length = perm.shape[1]
    row = lax.broadcasted_iota(jnp.int32, (length, length), 0)
    return (row == perm).astype(F32).astype(BF16)


def sketch_kernel(sketch_ref, perm_ref, kind_ref, values_ref, out_ref, coef_ref):
    pairs = kind_ref.shape[1]
    length = perm_ref.shape[1]
    one, two, cross = values_ref[0:1, :], values_ref[1:2, :], values_ref[2:3, :]
    twin = kind_ref[...] == 1
    det = one * two - cross * cross
    first = jnp.where(twin, two / det, 1.0 / one)
    second = jnp.where(twin, one / det, 1.0 / two)
    mixed = jnp.where(twin, -cross / det, 0.0)
    row = lax.broadcasted_iota(jnp.int32, (16, pairs), 0)
    stacked = jnp.where(row == 0, first, jnp.where(row == 1, second, mixed))
    pair = lax.broadcasted_iota(jnp.int32, (pairs, length), 0)
    lane = lax.broadcasted_iota(jnp.int32, (pairs, length), 1)
    even = (lane == 2 * pair).astype(F32).astype(BF16)
    odd = (lane == 2 * pair + 1).astype(F32).astype(BF16)
    at_even = onehot_dot(stacked, even, ((1,), (0,)))
    at_odd = onehot_dot(stacked, odd, ((1,), (0,)))
    diag = at_even[0:1] + at_odd[1:2]
    off = at_even[2:3] + at_odd[2:3]
    coef_ref[0:1, :] = diag
    coef_ref[1:2, :] = off
    scaled = pair_scale(sketch_ref[...], diag, off)
    placed = onehot_dot(scaled, selector_of(perm_ref[...]), ((1,), (1,)))
    chips, _, width = out_ref.shape
    for chip in range(chips):
        out_ref[chip] = placed[:, chip * width : (chip + 1) * width]


def stages(size):
    bits = []
    bit = size // 2
    while bit:
        bits.append(bit)
        bit //= 2
    return bits


def codes(size):
    order = [0]
    for bit in stages(size):
        order = order + [code ^ bit for code in order]
    return order


def stack_kernel(*refs):
    piece_refs, out_ref = refs[:-1], refs[-1]
    at = 0
    for piece_ref in piece_refs:
        out_ref[at : at + piece_ref.shape[0]] = piece_ref[...]
        at += piece_ref.shape[0]


def stack(*pieces):
    total = sum(piece.shape[0] for piece in pieces)
    return call(stack_kernel, shape(total, *pieces[0].shape[1:]), *pieces)


def gather(x, size, send):
    pieces = [x]
    for bit in stages(size):
        held = pieces[0] if len(pieces) == 1 else stack(*pieces)
        pieces = [held, send(held, bit)]
    return pieces


def entries(refs, size):
    order = codes(size)
    at = 0
    for ref in refs:
        for t in range(ref.shape[0]):
            yield order[at], ref, t
            at += 1


def lanes(ref, *index):
    low, high = index[-2:]
    lead = index[:-2]
    return jnp.concatenate(
        [ref[(chip, *lead, slice(low, high))] for chip in range(ref.shape[0])], axis=1
    )


def load_kernel(*refs):
    count = (len(refs) - 13) // 2
    packed, sources, (out_ref, cols_ref) = refs[:5], refs[5 : 5 + count], refs[5 + count : 7 + count]
    targets, buffers, sems = refs[7 + count : 7 + 2 * count], refs[7 + 2 * count : -1], refs[-1]
    core = lax.axis_index("col") % 2
    pairs = list(zip(packed, buffers))
    for source, target in zip(sources, targets):
        pairs.append((source.at[core] if len(source.shape) == 3 else source, target))
    copies = [
        pltpu.make_async_copy(source, target, sems.at[n])
        for n, (source, target) in enumerate(pairs)
    ]
    for copy in copies:
        copy.start()
    for copy in copies[:5]:
        copy.wait()
    row_basis_ref, row_coeff_ref, pivot_ref, col_basis_ref, col_scaled_ref = buffers
    rank = row_basis_ref.shape[1]
    half = rank // 2
    part = row_basis_ref.shape[2]
    for tile in range(2):
        where = slice(tile * part, (tile + 1) * part)
        out_ref[0, :rank, where] = row_basis_ref[tile]
        out_ref[0, rank : 2 * rank, where] = row_coeff_ref[tile]
        out_ref[0, 2 * rank :, where] = pivot_ref[tile * half : (tile + 1) * half]
    for col in range(col_basis_ref.shape[0]):
        base = 2 * col * rank
        cols_ref[0, base : base + rank] = col_basis_ref[col]
        cols_ref[0, base + rank : base + 2 * rank] = col_scaled_ref[col]
    for copy in copies[5:]:
        copy.wait()


def partial_kernel(sketch_ref, own_ref, other_ref, out_ref, panel_ref):
    core = lax.axis_index("col") % 2
    chip = lax.axis_index("col") // 2
    part = own_ref.shape[0]
    panel_ref[pl.ds(pl.multiple_of(core * part, part), part), :] = own_ref[...]
    panel_ref[pl.ds(pl.multiple_of((1 - core) * part, part), part), :] = other_ref[core]
    out_ref[...] = dot_nn(sketch_ref[chip], panel_ref[...])


def add_kernel(left_ref, right_ref, out_ref):
    out_ref[...] = left_ref[...] + right_ref[...]


def prepare_kernel(chips, pivot_ref, *refs):
    count = (len(refs) - 5) // 2
    own_refs, other_refs = refs[:count], refs[count : 2 * count]
    sketch_ref, panel_ref, factors_ref, corr_ref, updated_ref = refs[2 * count :]
    core = lax.axis_index("col") % 2
    chip = lax.axis_index("col") // 2
    rank = pivot_ref.shape[0]
    part = own_refs[0].shape[2] // 2
    for (code, own_ref, t), (_, other_ref, u) in zip(
        entries(own_refs, chips), entries(other_refs, chips)
    ):
        mine, theirs = own_ref[t], other_ref[u]
        for tile in range(2):
            where = slice(tile * part, (tile + 1) * part)
            left = jnp.where(core == 0, mine[:, where], theirs[:, where])
            right = jnp.where(core == 0, theirs[:, where], mine[:, where])
            factors_ref[chip ^ code, tile] = jnp.concatenate([left, right], axis=1)
    xrow = lanes(factors_ref, core, 0, rank)
    yrow = lanes(factors_ref, core, rank, 2 * rank)
    pbasis = jnp.concatenate(
        [lanes(factors_ref, tile, 2 * rank, 2 * rank + rank // 2) for tile in range(2)], axis=0
    )
    pcore = dot_nt(yrow, pivot_ref[...])
    lifted = dot_nn(pcore, pbasis)
    sketched = lanes(sketch_ref, 0, rank)
    corr_ref[...] = dot_nn(dot_nt(sketched, lifted), xrow)
    local = jnp.concatenate(
        [factors_ref[chip, tile, 2 * rank : 2 * rank + rank // 2, :] for tile in range(2)], axis=0
    )
    lifted = dot_nn(pcore, local)
    updated_ref[...] = panel_ref[...] - dot_nn(lifted.T, xrow)


def gram_kernel(left_ref, right_ref, corr_ref, updated_ref, range_ref, gram_ref, proj_ref):
    ranges = (left_ref[...] + right_ref[...]) - corr_ref[...]
    range_ref[...] = ranges
    proj_ref[0] = dot_nt(ranges, updated_ref[...])
    gram_ref[...] = dot_nt(ranges, ranges) / ranges.shape[1]


def factor_kernel(gram_ref, range_ref, out_ref):
    rank = gram_ref.shape[0]
    group = 8
    wide = (group, 2 * rank)
    row = lax.broadcasted_iota(jnp.int32, (group, rank), 0)
    col = lax.broadcasted_iota(jnp.int32, (group, rank), 1)
    work = [
        jnp.concatenate(
            [gram_ref[base : base + group], (row + base == col).astype(F32)], axis=1
        )
        for base in range(0, rank, group)
    ]
    rows = lax.broadcasted_iota(jnp.int32, wide, 0)

    def spread(x, lane):
        return jnp.broadcast_to(x[:, lane : lane + 1], wide)

    def pair(top, low, first, cross, second):
        det = first * second - cross * cross
        scale = 1.0 / det
        over = lambda x, y: ((x * second - y * cross) * scale, (y * first - x * cross) * scale)
        root = lax.rsqrt(first)
        done = (top * root, (low - top * (cross / first)) * (lax.rsqrt(det) * (first * root)))
        return over, done

    final = []
    for step in range(0, rank, 4):
        at, inner = divmod(step, group)
        one, two, three, four = [
            jnp.broadcast_to(work[at][inner + n : inner + n + 1], wide) for n in range(4)
        ]
        p11, p12, p13, p14 = [spread(one, step + n) for n in range(4)]
        p22, p23, p24 = [spread(two, step + n) for n in range(1, 4)]
        p33, p34, p44 = spread(three, step + 2), spread(three, step + 3), spread(four, step + 3)
        over, done = pair(one, two, p11, p12, p22)
        u1, u2 = over(one, two)
        u13, u23 = over(p13, p23)
        u14, u24 = over(p14, p24)
        three = three - (p13 * u1 + p23 * u2)
        four = four - (p14 * u1 + p24 * u2)
        over, more = pair(
            three,
            four,
            p33 - (p13 * u13 + p23 * u23),
            p34 - (p13 * u14 + p23 * u24),
            p44 - (p14 * u14 + p24 * u24),
        )
        u3, u4 = over(three, four)
        for index in range(at if inner == 0 else at + 1, len(work)):
            held = work[index]
            h1, h2, h3, h4 = [spread(held, step + n) for n in range(4)]
            h3 = h3 - (h1 * u13 + h2 * u23)
            h4 = h4 - (h1 * u14 + h2 * u24)
            work[index] = held - ((h1 * u1 + h2 * u2) + (h3 * u3 + h4 * u4))
        for n, value in enumerate(done + more):
            if inner + n == 0:
                final.append(value)
            else:
                final[at] = jnp.where(rows >= inner + n, value, final[at])
    inverse = jnp.concatenate([block[:, rank:] for block in final], axis=0)
    size = range_ref.shape[1]
    out_ref[:, :size] = dot_nn(inverse, range_ref[...])
    out_ref[:, size : size + rank] = inverse


def coeff_kernel(chips, own_ref, other_ref, perm_ref, coef_ref, *refs):
    count = (len(refs) - 3) // 2
    own_refs, other_refs = refs[:count], refs[count : 2 * count]
    basis_ref, coeff_ref, stack_ref = refs[2 * count :]
    core = lax.axis_index("col") % 2
    chip = lax.axis_index("col") // 2
    rank = own_ref.shape[0]
    size = perm_ref.shape[1]
    projected = []
    for source, pieces in ((own_ref, own_refs), (other_ref, other_refs)):
        for code, ref, t in entries(pieces, chips):
            stack_ref[chip ^ code] = ref[t]
        projected.append(dot_nn(source[:, size : size + rank], lanes(stack_ref, 0, rank)))
    both = jnp.concatenate(projected, axis=0)
    permuted = onehot_dot(both, selector_of(perm_ref[...]), ((1,), (0,)))
    result = pair_scale(permuted, coef_ref[0:1, :], coef_ref[1:2, :]) / jnp.sqrt(jnp.float32(size))
    basis_ref[core] = own_ref[:, :size]
    basis_ref[1 - core] = other_ref[:, :size]
    coeff_ref[core] = result[:rank]
    coeff_ref[1 - core] = result[rank:]


def dot3(left, right, dims):
    high, low = left.astype(BF16), None
    low = (left - high.astype(F32)).astype(BF16)
    top = right.astype(BF16)
    rest = (right - top.astype(F32)).astype(BF16)
    dot = lambda a, b: lax.dot_general(a, b, (dims, ((), ())), preferred_element_type=F32)
    return dot(high, top) + (dot(low, top) + dot(high, rest))


def left_kernel(nrow, factors_ref, *refs):
    col_refs, (left_ref, right_ref, cols_ref) = refs[:-3], refs[-3:]
    row = lax.axis_index("row")
    tiles, ncols, _, deep = left_ref.shape
    rank = deep // 3
    for code, ref, t in entries(col_refs, nrow):
        cols_ref[row ^ code] = ref[t]
    for col in range(ncols):
        basis = lanes(cols_ref, 2 * col * rank, (2 * col + 1) * rank)
        high = basis.astype(BF16)
        right_ref[col, :rank, :] = high
        right_ref[col, rank : 2 * rank, :] = high
        right_ref[col, 2 * rank :, :] = (basis - high.astype(F32)).astype(BF16)
    scaled = jnp.concatenate(
        [lanes(cols_ref, (2 * col + 1) * rank, (2 * col + 2) * rank) for col in range(ncols)],
        axis=0,
    )
    yrows = jnp.concatenate(
        [lanes(factors_ref, tile, rank, 2 * rank) for tile in range(tiles)], axis=0
    )
    core = dot3(scaled, yrows, ((1,), (1,)))
    for tile in range(tiles):
        left = dot3(
            core[:, tile * rank : (tile + 1) * rank],
            lanes(factors_ref, tile, 0, rank),
            ((1,), (0,)),
        ).T
        high = left.astype(BF16)
        low = (left - high.astype(F32)).astype(BF16)
        for col in range(ncols):
            part = slice(col * rank, (col + 1) * rank)
            left_ref[tile, col, :, :rank] = high[:, part]
            left_ref[tile, col, :, rank : 2 * rank] = low[:, part]
            left_ref[tile, col, :, 2 * rank :] = high[:, part]


def trail_kernel(trail_ref, left_ref, right_ref, out_ref):
    tile = pl.program_id(0)
    ncols, _, width = right_ref.shape
    size = left_ref.shape[2]
    groups = width // 128
    for col in range(ncols):
        change = jnp.dot(left_ref[tile, col], right_ref[col], preferred_element_type=F32)
        for group in range(groups):
            where = pl.ds(col * groups + group, size, stride=ncols * groups)
            out_ref[0, where, :] = (
                trail_ref[0, where, :] - change[:, group * 128 : (group + 1) * 128]
            )


def left_call(nrow, tiles, size, factors, cols):
    rank = factors.shape[2] * 2 // 5
    ncols = cols[0].shape[1] // (2 * rank)
    return call(
        lambda *refs: left_kernel(nrow, *refs),
        [
            jax.ShapeDtypeStruct((tiles, ncols, size, 3 * rank), BF16),
            jax.ShapeDtypeStruct((ncols, 3 * rank, nrow * cols[0].shape[2]), BF16),
        ],
        factors,
        *cols,
        scratch=[pltpu.VMEM((nrow, *cols[0].shape[1:]), F32)],
        flops=1 << 26,
    )


def trail_call(trail, left, right):
    tiles, _, size, ncols, _, width = trail.shape
    groups = width // 128
    view = trail.reshape(tiles, size * ncols * groups, 128)
    block = pl.BlockSpec((1, size * ncols * groups, 128), lambda a: (a, 0, 0))
    vmem = pl.BlockSpec(memory_space=pltpu.VMEM)
    out = pl.pallas_call(
        trail_kernel,
        out_shape=jax.ShapeDtypeStruct(view.shape, F32),
        grid=(tiles,),
        in_specs=[block, vmem, vmem],
        out_specs=block,
        cost_estimate=pl.CostEstimate(
            flops=2 * tiles * ncols * size * left.shape[3] * width,
            transcendentals=0,
            bytes_accessed=2 * view.size * 4,
        ),
        compiler_params=pltpu.CompilerParams(vmem_limit_bytes=20 << 20),
        name="trail",
    )(view, left, right)
    return out.reshape(trail.shape)


def body_of(nrow, ncol):
    chips = ncol // 2
    assert chips & (chips - 1) == 0 and nrow & (nrow - 1) == 0

    def to_core(x):
        return lax.ppermute(x, "col", [(i, i ^ 1) for i in range(ncol)])

    def to_chip(x, bit):
        return lax.ppermute(x, "col", [(i, i ^ (2 * bit)) for i in range(ncol)])

    def to_row(x, bit):
        return lax.ppermute(x, "row", [(i, i ^ bit) for i in range(nrow)])

    def body(
        trail,
        panel,
        row_basis,
        row_coeff,
        col_basis,
        col_scaled,
        pivot_basis,
        pivot_scaled,
        sketch,
        perm,
        pair_kind,
        pivot_values,
    ):
        _, _, size, part = panel.shape
        rank = sketch.shape[0]
        half = rank // 2
        width = 2 * part
        panel_t = jnp.transpose(panel[:, 0], (0, 2, 1))
        perm_row = perm.reshape(1, -1)
        panel_other = to_core(panel_t)
        inputs = (sketch, perm_row, pair_kind.reshape(1, -1), pivot_values, pivot_scaled)
        factors, columns, panel_own, *loaded, pivot_loaded = call(
            load_kernel,
            [
                shape(1, 2 * rank + half, width),
                shape(1, 2 * rank * col_basis.shape[0], col_basis.shape[3]),
                shape(part, size),
                *[jax.ShapeDtypeStruct(x.shape, x.dtype) for x in inputs],
            ],
            row_basis[:, 0],
            row_coeff[:, 0],
            pivot_basis,
            col_basis[:, 0],
            col_scaled[:, 0],
            panel_t,
            *inputs,
            kept=6 + len(inputs),
            scratch=[
                *[
                    pltpu.VMEM((x.shape[0], *x.shape[2:]), F32)
                    for x in (row_basis, row_coeff)
                ],
                pltpu.VMEM(pivot_basis.shape, F32),
                *[
                    pltpu.VMEM((x.shape[0], *x.shape[2:]), F32)
                    for x in (col_basis, col_scaled)
                ],
                pltpu.SemaphoreType.DMA((6 + len(inputs),)),
            ],
        )
        sketch_t, coef = call(
            sketch_kernel, [shape(chips, rank, width), shape(2, size)], *loaded, flops=1 << 28
        )
        total, panel_mine = call(
            partial_kernel,
            [shape(rank, size), shape(width, size)],
            sketch_t,
            panel_own,
            panel_other,
            flops=1 << 26,
        )
        own = gather(factors, chips, to_chip)
        cols = gather(columns, nrow, to_row)
        bits = stages(chips)[::-1]
        for bit in bits[:-1]:
            remote = to_chip(total, bit)
            total = call(add_kernel, shape(rank, size), total, remote)
        remote = to_chip(total, bits[-1])
        other = []
        for piece in own:
            other.append(to_core(piece))
        factors_all, corr, updated = call(
            lambda *refs: prepare_kernel(chips, *refs),
            [shape(chips, 2, 2 * rank + half, width), shape(rank, size), shape(width, size)],
            pivot_loaded,
            *own,
            *other,
            sketch_t,
            panel_mine,
            flops=1 << 26,
        )
        ranges, gram, proj = call(
            gram_kernel,
            [shape(rank, size), shape(rank, rank), shape(1, rank, width)],
            total,
            remote,
            corr,
            updated,
            flops=1 << 26,
        )
        projs = gather(proj, chips, to_chip)
        basis = call(factor_kernel, shape(rank, size + 128), gram, ranges, flops=1 << 28)
        basis_other = to_core(basis)
        left, right = left_call(nrow, 2, size, factors_all, cols)
        trail_out = trail_call(trail, left, right)
        projs_other = []
        for piece in projs:
            projs_other.append(to_core(piece))
        basis_out, coeff_out = call(
            lambda *refs: coeff_kernel(chips, *refs),
            [shape(2, rank, size)] * 2,
            basis,
            basis_other,
            loaded[1],
            coef,
            *projs,
            *projs_other,
            scratch=[pltpu.VMEM((chips, rank, width), F32)],
            flops=1 << 28,
        )
        return (trail_out, basis_out[:, None], coeff_out[:, None])

    return body


def solution(mesh):
    step = body_of(mesh.shape["row"], mesh.shape["col"])

    return jax.shard_map(
        step,
        mesh=mesh,
        in_specs=(
            P(None, "row", None, None, "col", None),
            P(None, "row", None, "col"),
            P(None, "row", None, "col"),
            P(None, "row", None, "col"),
            P(None, "col", None, "row"),
            P(None, "col", None, "row"),
            P(None, "col"),
            P(),
            P(),
            P(),
            P(),
            P(),
        ),
        out_specs=(
            P(None, "row", None, None, "col", None),
            P(None, "row", None, None),
            P(None, "row", None, None),
        ),
        check_vma=False,
    )
```

```python
import jax
import jax.numpy as jnp
from jax import lax
from jax.experimental import pallas as pl
from jax.experimental.pallas import tpu as pltpu
from jax.sharding import PartitionSpec as P


F32 = jnp.float32
BF16 = jnp.bfloat16
HIGHEST = lax.Precision.HIGHEST


def dot_nn(left, right):
    return lax.dot_general(
        left, right, (((1,), (0,)), ((), ())), precision=HIGHEST, preferred_element_type=F32
    )


def dot_nt(left, right):
    return lax.dot_general(
        left, right, (((1,), (1,)), ((), ())), precision=HIGHEST, preferred_element_type=F32
    )


def split3(x):
    high = x.astype(BF16)
    rest = x - high.astype(F32)
    mid = rest.astype(BF16)
    low = (rest - mid.astype(F32)).astype(BF16)
    return high, mid, low


def onehot_dot(x, onehot, dims):
    rows = x.shape[0]
    parts = lax.dot_general(
        jnp.concatenate(split3(x), axis=0),
        onehot,
        (dims, ((), ())),
        preferred_element_type=F32,
    )
    return parts[:rows] + (parts[rows : 2 * rows] + parts[2 * rows :])


def call(kernel, outs, *args, fetched=0, kept=0, placed=0, scratch=(), flops=0):
    vmem = pl.BlockSpec(memory_space=pltpu.VMEM)
    hbm = pl.BlockSpec(memory_space=pltpu.HBM)
    many = isinstance(outs, (list, tuple))
    args = [
        pltpu.with_memory_space_constraint(x, pltpu.HBM) if n < fetched + kept else x
        for n, x in enumerate(args)
    ]
    buffers = [pltpu.VMEM(x.shape, x.dtype) for x in args[:fetched]]

    def wrapped(*refs):
        refs = list(refs)
        extra = refs[len(refs) - fetched - 1 :] if fetched else []
        if fetched:
            refs = refs[: len(refs) - fetched - 1]
            copies = [
                pltpu.make_async_copy(refs[n], extra[n], extra[-1].at[n]) for n in range(fetched)
            ]
            for copy in copies:
                copy.start()
            for copy in copies:
                copy.wait()
            refs[:fetched] = extra[:fetched]
        kernel(*refs)

    scratch = list(scratch)
    if fetched:
        scratch += buffers + [pltpu.SemaphoreType.DMA((fetched,))]
    return pl.pallas_call(
        wrapped,
        out_shape=outs,
        in_specs=[hbm] * (fetched + kept) + [vmem] * (len(args) - fetched - kept),
        out_specs=[hbm] * placed + [vmem] * (len(outs) - placed) if many else vmem,
        scratch_shapes=scratch,
        cost_estimate=pl.CostEstimate(flops=flops, transcendentals=0, bytes_accessed=1 << 20),
        compiler_params=pltpu.CompilerParams(vmem_limit_bytes=8 << 20),
    )(*args)


def shape(*dims):
    return jax.ShapeDtypeStruct(dims, F32)


def pair_scale(rows, diag, off):
    length = rows.shape[1]
    lane = lax.broadcasted_iota(jnp.int32, rows.shape, 1)
    after = pltpu.roll(rows, length - 1, 1)
    before = pltpu.roll(rows, 1, 1)
    return rows * diag + jnp.where(lane % 2 == 0, after, before) * off


def selector_of(perm):
    length = perm.shape[1]
    row = lax.broadcasted_iota(jnp.int32, (length, length), 0)
    return (row == perm).astype(F32).astype(BF16)


def sketch_kernel(
    sketch_ref, perm_ref, kind_ref, values_ref, out_ref, coef_ref, selector_ref
):
    pairs = kind_ref.shape[1]
    length = perm_ref.shape[1]
    one, two, cross = values_ref[0:1, :], values_ref[1:2, :], values_ref[2:3, :]
    twin = kind_ref[...] == 1
    det = one * two - cross * cross
    first = jnp.where(twin, two / det, 1.0 / one)
    second = jnp.where(twin, one / det, 1.0 / two)
    mixed = jnp.where(twin, -cross / det, 0.0)
    row = lax.broadcasted_iota(jnp.int32, (16, pairs), 0)
    stacked = jnp.where(row == 0, first, jnp.where(row == 1, second, mixed))
    pair = lax.broadcasted_iota(jnp.int32, (pairs, length), 0)
    lane = lax.broadcasted_iota(jnp.int32, (pairs, length), 1)
    even = (lane == 2 * pair).astype(F32).astype(BF16)
    odd = (lane == 2 * pair + 1).astype(F32).astype(BF16)
    at_even = onehot_dot(stacked, even, ((1,), (0,)))
    at_odd = onehot_dot(stacked, odd, ((1,), (0,)))
    diag = at_even[0:1] + at_odd[1:2]
    off = at_even[2:3] + at_odd[2:3]
    coef_ref[0:1, :] = diag
    coef_ref[1:2, :] = off
    scaled = pair_scale(sketch_ref[...], diag, off)
    selector = selector_of(perm_ref[...])
    selector_ref[...] = selector
    placed = onehot_dot(scaled, selector, ((1,), (1,)))
    chips, _, width = out_ref.shape
    for chip in range(chips):
        out_ref[chip] = placed[:, chip * width : (chip + 1) * width]


def stages(size):
    bits = []
    bit = size // 2
    while bit:
        bits.append(bit)
        bit //= 2
    return bits


def codes(bits, start=(0,)):
    order = list(start)
    for bit in bits:
        order = order + [code ^ bit for code in order]
    return order


def stack_kernel(*refs):
    piece_refs, out_ref = refs[:-1], refs[-1]
    at = 0
    for piece_ref in piece_refs:
        out_ref[at : at + piece_ref.shape[0]] = piece_ref[...]
        at += piece_ref.shape[0]


def stack(*pieces):
    total = sum(piece.shape[0] for piece in pieces)
    return call(stack_kernel, shape(total, *pieces[0].shape[1:]), *pieces)


def gather(x, bits, send):
    pieces = [x]
    for bit in bits:
        held = pieces[0] if len(pieces) == 1 else stack(*pieces)
        pieces = [held, send(held, bit)]
    return pieces


def entries(refs, order):
    at = 0
    for ref in refs:
        for t in range(ref.shape[0]):
            yield order[at], ref, t
            at += 1


def lanes(ref, *index):
    low, high = index[-2:]
    lead = index[:-2]
    return jnp.concatenate(
        [ref[(chip, *lead, slice(low, high))] for chip in range(ref.shape[0])], axis=1
    )


def load_kernel(*refs):
    count = (len(refs) - 13) // 2
    packed, sources, (out_ref, cols_ref) = refs[:5], refs[5 : 5 + count], refs[5 + count : 7 + count]
    targets, buffers, sems = refs[7 + count : 7 + 2 * count], refs[7 + 2 * count : -1], refs[-1]
    core = lax.axis_index("col") % 2
    pairs = list(zip(packed, buffers))
    for n, (source, target) in enumerate(zip(sources, targets)):
        pairs.append((source.at[core] if n == 0 else source, target))
    copies = [
        pltpu.make_async_copy(source, target, sems.at[n])
        for n, (source, target) in enumerate(pairs)
    ]
    for copy in copies:
        copy.start()
    for copy in copies[:5]:
        copy.wait()
    row_basis_ref, row_coeff_ref, pivot_ref, col_basis_ref, col_scaled_ref = buffers
    rank = row_basis_ref.shape[1]
    half = rank // 2
    part = row_basis_ref.shape[2]
    for tile in range(2):
        where = slice(tile * part, (tile + 1) * part)
        out_ref[0, :rank, where] = row_basis_ref[tile]
        out_ref[0, rank : 2 * rank, where] = row_coeff_ref[tile]
        out_ref[0, 2 * rank :, where] = pivot_ref[tile * half : (tile + 1) * half]
    for col in range(col_basis_ref.shape[0]):
        base = 2 * col * rank
        cols_ref[0, base : base + rank] = col_basis_ref[col]
        cols_ref[0, base + rank : base + 2 * rank] = col_scaled_ref[col]
    for copy in copies[5:]:
        copy.wait()


def join_kernel(own_ref, other_ref, out_ref):
    core = lax.axis_index("col") % 2
    part = own_ref.shape[0]
    out_ref[pl.ds(pl.multiple_of(core * part, part), part), :] = own_ref[...]
    out_ref[pl.ds(pl.multiple_of((1 - core) * part, part), part), :] = other_ref[core]


def partial_kernel(sketch_ref, own_ref, near_ref, out_ref):
    chip = lax.axis_index("col") // 2
    out_ref[...] = dot_nn(sketch_ref[chip], own_ref[...]) + dot_nn(
        sketch_ref[chip ^ 1], near_ref[...]
    )


def add_kernel(left_ref, right_ref, out_ref):
    out_ref[...] = left_ref[...] + right_ref[...]


def prepare_kernel(order, pivot_ref, *refs):
    count = (len(refs) - 6) // 2
    own_refs, other_refs = refs[:count], refs[count : 2 * count]
    sketch_ref, *panel_refs, factors_ref, corr_ref, updated_ref = refs[2 * count :]
    core = lax.axis_index("col") % 2
    chip = lax.axis_index("col") // 2
    rank = pivot_ref.shape[0]
    part = own_refs[0].shape[2] // 2
    for (code, own_ref, t), (_, other_ref, u) in zip(
        entries(own_refs, order), entries(other_refs, order)
    ):
        mine, theirs = own_ref[t], other_ref[u]
        for tile in range(2):
            where = slice(tile * part, (tile + 1) * part)
            left = jnp.where(core == 0, mine[:, where], theirs[:, where])
            right = jnp.where(core == 0, theirs[:, where], mine[:, where])
            factors_ref[chip ^ code, tile] = jnp.concatenate([left, right], axis=1)
    xrow = lanes(factors_ref, core, 0, rank)
    yrow = lanes(factors_ref, core, rank, 2 * rank)
    pbasis = jnp.concatenate(
        [lanes(factors_ref, tile, 2 * rank, 2 * rank + rank // 2) for tile in range(2)], axis=0
    )
    pcore = dot_nt(yrow, pivot_ref[...])
    mixed = dot_nt(dot_nt(lanes(sketch_ref, 0, rank), pbasis), pcore)
    local = jnp.concatenate(
        [
            jnp.concatenate(
                [
                    factors_ref[chip ^ slot, tile, 2 * rank : 2 * rank + rank // 2, :]
                    for tile in range(2)
                ],
                axis=0,
            )
            for slot in range(len(panel_refs))
        ],
        axis=1,
    )
    sides = jnp.concatenate([mixed, dot_nn(pcore, local).T], axis=0)
    change = dot_nn(sides, xrow)
    corr_ref[...] = change[:rank]
    at = rank
    for slot, panel_ref in enumerate(panel_refs):
        deep = panel_ref.shape[0]
        updated_ref[slot] = panel_ref[...] - change[at : at + deep]
        at += deep


def gram_kernel(left_ref, right_ref, corr_ref, updated_ref, range_ref, gram_ref, proj_ref):
    ranges = (left_ref[...] + right_ref[...]) - corr_ref[...]
    range_ref[...] = ranges
    slots, width, size = updated_ref.shape
    products = dot_nt(
        ranges, jnp.concatenate([updated_ref[slot] for slot in range(slots)] + [ranges], axis=0)
    )
    for slot in range(slots):
        proj_ref[slot] = products[:, slot * width : (slot + 1) * width]
    gram_ref[...] = products[:, slots * width :] / size


def factor_kernel(gram_ref, range_ref, out_ref):
    rank = gram_ref.shape[0]
    group = 8
    wide = (group, 2 * rank)
    row = lax.broadcasted_iota(jnp.int32, (group, rank), 0)
    col = lax.broadcasted_iota(jnp.int32, (group, rank), 1)
    work = [
        jnp.concatenate(
            [gram_ref[base : base + group], (row + base == col).astype(F32)], axis=1
        )
        for base in range(0, rank, group)
    ]
    rows = lax.broadcasted_iota(jnp.int32, wide, 0)

    def spread(x, lane):
        return jnp.broadcast_to(x[:, lane : lane + 1], wide)

    def pair(top, low, first, cross, second):
        det = first * second - cross * cross
        scale = 1.0 / det
        over = lambda x, y: ((x * second - y * cross) * scale, (y * first - x * cross) * scale)
        root = lax.rsqrt(first)
        done = (top * root, (low - top * (cross / first)) * (lax.rsqrt(det) * (first * root)))
        return over, done

    final = []
    for step in range(0, rank, 4):
        at, inner = divmod(step, group)
        one, two, three, four = [
            jnp.broadcast_to(work[at][inner + n : inner + n + 1], wide) for n in range(4)
        ]
        p11, p12, p13, p14 = [spread(one, step + n) for n in range(4)]
        p22, p23, p24 = [spread(two, step + n) for n in range(1, 4)]
        p33, p34, p44 = spread(three, step + 2), spread(three, step + 3), spread(four, step + 3)
        over, done = pair(one, two, p11, p12, p22)
        u1, u2 = over(one, two)
        u13, u23 = over(p13, p23)
        u14, u24 = over(p14, p24)
        three = three - (p13 * u1 + p23 * u2)
        four = four - (p14 * u1 + p24 * u2)
        over, more = pair(
            three,
            four,
            p33 - (p13 * u13 + p23 * u23),
            p34 - (p13 * u14 + p23 * u24),
            p44 - (p14 * u14 + p24 * u24),
        )
        u3, u4 = over(three, four)
        for index in range(at if inner == 0 else at + 1, len(work)):
            held = work[index]
            h1, h2, h3, h4 = [spread(held, step + n) for n in range(4)]
            h3 = h3 - (h1 * u13 + h2 * u23)
            h4 = h4 - (h1 * u14 + h2 * u24)
            work[index] = held - ((h1 * u1 + h2 * u2) + (h3 * u3 + h4 * u4))
        for n, value in enumerate(done + more):
            if inner + n == 0:
                final.append(value)
            else:
                final[at] = jnp.where(rows >= inner + n, value, final[at])
    inverse = jnp.concatenate([block[:, rank:] for block in final], axis=0)
    size = range_ref.shape[1]
    out_ref[:, :size] = dot_nn(inverse, range_ref[...])
    out_ref[:, size : size + rank] = inverse


def coeff_of(order, basis_ref, selector_ref, coef_ref, piece_refs, stack_ref):
    chip = lax.axis_index("col") // 2
    rank = basis_ref.shape[0]
    size = selector_ref.shape[1]
    for code, ref, t in entries(piece_refs, order):
        stack_ref[chip ^ code] = ref[t]
    projected = dot_nn(basis_ref[:, size : size + rank], lanes(stack_ref, 0, rank))
    permuted = onehot_dot(projected, selector_ref[...], ((1,), (0,)))
    return pair_scale(permuted, coef_ref[0:1, :], coef_ref[1:2, :]) / jnp.sqrt(jnp.float32(size))


def coeff_kernel(order, basis_ref, other_ref, selector_ref, coef_ref, *refs):
    core = lax.axis_index("col") % 2
    basis_out_ref, out_ref, stack_ref, sems = refs[-4:]
    size = selector_ref.shape[1]
    copies = [
        pltpu.make_async_copy(source.at[:, :size], basis_out_ref.at[tile], sems.at[n])
        for n, (source, tile) in enumerate(((basis_ref, core), (other_ref, 1 - core)))
    ]
    for copy in copies:
        copy.start()
    out_ref[...] = coeff_of(order, basis_ref, selector_ref, coef_ref, refs[:-4], stack_ref)
    for copy in copies:
        copy.wait()


def finish_kernel(order, basis_ref, selector_ref, coef_ref, own_ref, *refs):
    core = lax.axis_index("col") % 2
    out_ref, stack_ref = refs[-2:]
    out_ref[core] = own_ref[...]
    out_ref[1 - core] = coeff_of(order, basis_ref, selector_ref, coef_ref, refs[:-2], stack_ref)


def dot3(left, right, dims):
    high, low = left.astype(BF16), None
    low = (left - high.astype(F32)).astype(BF16)
    top = right.astype(BF16)
    rest = (right - top.astype(F32)).astype(BF16)
    dot = lambda a, b: lax.dot_general(a, b, (dims, ((), ())), preferred_element_type=F32)
    return dot(high, top) + (dot(low, top) + dot(high, rest))


def left_kernel(order, factors_ref, *refs):
    col_refs, (left_ref, right_ref, cols_ref) = refs[:-3], refs[-3:]
    row = lax.axis_index("row")
    tiles, ncols, _, deep = left_ref.shape
    rank = deep // 3
    for code, ref, t in entries(col_refs, order):
        cols_ref[row ^ code] = ref[t]
    for col in range(ncols):
        basis = lanes(cols_ref, 2 * col * rank, (2 * col + 1) * rank)
        high = basis.astype(BF16)
        right_ref[col, :rank, :] = high
        right_ref[col, rank : 2 * rank, :] = high
        right_ref[col, 2 * rank :, :] = (basis - high.astype(F32)).astype(BF16)
    scaled = jnp.concatenate(
        [lanes(cols_ref, (2 * col + 1) * rank, (2 * col + 2) * rank) for col in range(ncols)],
        axis=0,
    )
    yrows = jnp.concatenate(
        [lanes(factors_ref, tile, rank, 2 * rank) for tile in range(tiles)], axis=0
    )
    core = dot3(scaled, yrows, ((1,), (1,)))
    for tile in range(tiles):
        left = dot3(
            core[:, tile * rank : (tile + 1) * rank],
            lanes(factors_ref, tile, 0, rank),
            ((1,), (0,)),
        ).T
        high = left.astype(BF16)
        low = (left - high.astype(F32)).astype(BF16)
        for col in range(ncols):
            part = slice(col * rank, (col + 1) * rank)
            left_ref[tile, col, :, :rank] = high[:, part]
            left_ref[tile, col, :, rank : 2 * rank] = low[:, part]
            left_ref[tile, col, :, 2 * rank :] = high[:, part]


def trail_kernel(trail_ref, left_ref, right_ref, out_ref, change_ref, held_ref, sems):
    tiles, ncols, size, _ = left_ref.shape
    groups = right_ref.shape[2] // 128
    step = ncols * groups
    chunks = sems.shape[1]
    rows = size // chunks
    copies = []
    for tile in range(tiles):
        for col in range(ncols):
            change_ref[col] = jnp.dot(
                left_ref[tile, col], right_ref[col], preferred_element_type=F32
            )
        for chunk in range(chunks):
            for col in range(ncols):
                for group in range(groups):
                    where = pl.ds(chunk * rows * step + col * groups + group, rows, stride=step)
                    held_ref[tile, where, :] = (
                        trail_ref[tile, where, :]
                        - change_ref[
                            col,
                            chunk * rows : (chunk + 1) * rows,
                            group * 128 : (group + 1) * 128,
                        ]
                    )
            part = pl.ds(chunk * rows * step, rows * step)
            copy = pltpu.make_async_copy(
                held_ref.at[tile, part], out_ref.at[tile, part], sems.at[tile, chunk]
            )
            copy.start()
            copies.append(copy)
    for copy in copies:
        copy.wait()


def left_call(nrow, order, tiles, size, factors, cols):
    rank = factors.shape[2] * 2 // 5
    ncols = cols[0].shape[1] // (2 * rank)
    return call(
        lambda *refs: left_kernel(order, *refs),
        [
            jax.ShapeDtypeStruct((tiles, ncols, size, 3 * rank), BF16),
            jax.ShapeDtypeStruct((ncols, 3 * rank, nrow * cols[0].shape[2]), BF16),
        ],
        factors,
        *cols,
        scratch=[pltpu.VMEM((nrow, *cols[0].shape[1:]), F32)],
        flops=1 << 26,
    )


def trail_call(trail, left, right, chunks=4):
    tiles, _, size, ncols, _, width = trail.shape
    rows = size * ncols * width // 128
    view = trail.reshape(tiles, rows, 128)
    vmem = pl.BlockSpec(memory_space=pltpu.VMEM)
    out = pl.pallas_call(
        trail_kernel,
        out_shape=jax.ShapeDtypeStruct(view.shape, F32),
        in_specs=[vmem] * 3,
        out_specs=pl.BlockSpec(memory_space=pltpu.HBM),
        scratch_shapes=[
            pltpu.VMEM((ncols, size, width), F32),
            pltpu.VMEM(view.shape, F32),
            pltpu.SemaphoreType.DMA((tiles, chunks)),
        ],
        cost_estimate=pl.CostEstimate(
            flops=2 * tiles * ncols * size * left.shape[3] * width,
            transcendentals=0,
            bytes_accessed=2 * view.size * 4,
        ),
        compiler_params=pltpu.CompilerParams(vmem_limit_bytes=20 << 20),
        name="trail",
    )(view, left, right)
    return out.reshape(trail.shape)


def body_of(nrow, ncol):
    chips = ncol // 2
    assert chips > 2 and chips & (chips - 1) == 0 and nrow & (nrow - 1) == 0

    def to_core(x):
        return lax.ppermute(x, "col", [(i, i ^ 1) for i in range(ncol)])

    def to_chip(x, bit):
        return lax.ppermute(x, "col", [(i, i ^ (2 * bit)) for i in range(ncol)])

    def to_row(x, bit):
        return lax.ppermute(x, "row", [(i, i ^ bit) for i in range(nrow)])

    def body(
        trail,
        panel,
        row_basis,
        row_coeff,
        col_basis,
        col_scaled,
        pivot_basis,
        pivot_scaled,
        sketch,
        perm,
        pair_kind,
        pivot_values,
    ):
        _, _, size, part = panel.shape
        rank = sketch.shape[0]
        half = rank // 2
        width = 2 * part
        panel_t = jnp.transpose(panel[:, 0], (0, 2, 1))
        perm_row = perm.reshape(1, -1)
        bits = stages(chips)
        order = codes(bits)
        pair_order = codes(bits[:-1], (0, 1))
        panel_other = to_core(panel_t)
        inputs = (sketch, perm_row, pair_kind.reshape(1, -1), pivot_values, pivot_scaled)
        packed = (row_basis[:, 0], row_coeff[:, 0], pivot_basis, col_basis[:, 0], col_scaled[:, 0])
        factors, columns, panel_own, *loaded, pivot_loaded = call(
            load_kernel,
            [
                shape(1, 2 * rank + half, width),
                shape(1, 2 * rank * col_basis.shape[0], col_basis.shape[3]),
                shape(part, size),
                *[jax.ShapeDtypeStruct(x.shape, x.dtype) for x in inputs],
            ],
            *packed,
            panel_t,
            *inputs,
            kept=6 + len(inputs),
            scratch=[
                *[pltpu.VMEM(x.shape, F32) for x in packed],
                pltpu.SemaphoreType.DMA((6 + len(inputs),)),
            ],
        )
        panel_mine = call(join_kernel, shape(width, size), panel_own, panel_other)
        near = to_chip(panel_mine, 1)
        own = gather(factors, bits, to_chip)
        cols = gather(columns, stages(nrow), to_row)
        sketch_t, coef, selector = call(
            sketch_kernel,
            [shape(chips, rank, width), shape(2, size), jax.ShapeDtypeStruct((size, size), BF16)],
            *loaded,
            flops=1 << 28,
        )
        total = call(partial_kernel, shape(rank, size), sketch_t, panel_mine, near, flops=1 << 26)
        sums = bits[:-1][::-1]
        for bit in sums[:-1]:
            remote = to_chip(total, bit)
            total = call(add_kernel, shape(rank, size), total, remote)
        remote = to_chip(total, sums[-1])
        other = []
        for piece in own:
            other.append(to_core(piece))
        factors_all, corr, updated = call(
            lambda *refs: prepare_kernel(order, *refs),
            [
                shape(chips, 2, 2 * rank + half, width),
                shape(rank, size),
                shape(2, width, size),
            ],
            pivot_loaded,
            *own,
            *other,
            sketch_t,
            panel_mine,
            near,
            flops=1 << 26,
        )
        ranges, gram, proj = call(
            gram_kernel,
            [shape(rank, size), shape(rank, rank), shape(2, rank, width)],
            total,
            remote,
            corr,
            updated,
            flops=1 << 26,
        )
        projs = gather(proj, bits[:-1], to_chip)
        basis = call(factor_kernel, shape(rank, size + 128), gram, ranges, flops=1 << 28)
        basis_other = to_core(basis)
        left, right = left_call(nrow, codes(stages(nrow)), 2, size, factors_all, cols)
        trail_out = trail_call(trail, left, right)
        projs_other = []
        for piece in projs:
            projs_other.append(to_core(piece))
        scratch = [pltpu.VMEM((chips, rank, width), F32)]
        basis_out, coeff = call(
            lambda *refs: coeff_kernel(pair_order, *refs),
            [shape(2, rank, size), shape(rank, size)],
            basis,
            basis_other,
            selector,
            coef,
            *projs,
            placed=1,
            scratch=[*scratch, pltpu.SemaphoreType.DMA((2,))],
            flops=1 << 28,
        )
        coeff_out = call(
            lambda *refs: finish_kernel(pair_order, *refs),
            shape(2, rank, size),
            basis_other,
            selector,
            coef,
            coeff,
            *projs_other,
            scratch=scratch,
            flops=1 << 28,
        )
        return (trail_out, basis_out[:, None], coeff_out[:, None])

    return body


def solution(mesh):
    step = body_of(mesh.shape["row"], mesh.shape["col"])

    return jax.shard_map(
        step,
        mesh=mesh,
        in_specs=(
            P(None, "row", None, None, "col", None),
            P(None, "row", None, "col"),
            P(None, "row", None, "col"),
            P(None, "row", None, "col"),
            P(None, "col", None, "row"),
            P(None, "col", None, "row"),
            P(None, "col"),
            P(),
            P(),
            P(),
            P(),
            P(),
        ),
        out_specs=(
            P(None, "row", None, None, "col", None),
            P(None, "row", None, None),
            P(None, "row", None, None),
        ),
        check_vma=False,
    )
```

```python
import jax
import jax.numpy as jnp
from jax import lax
from jax.experimental import pallas as pl
from jax.experimental.pallas import tpu as pltpu
from jax.sharding import PartitionSpec as P


F32 = jnp.float32
BF16 = jnp.bfloat16
HIGHEST = lax.Precision.HIGHEST


def dot_nn(left, right):
    return lax.dot_general(
        left, right, (((1,), (0,)), ((), ())), precision=HIGHEST, preferred_element_type=F32
    )


def dot_nt(left, right):
    return lax.dot_general(
        left, right, (((1,), (1,)), ((), ())), precision=HIGHEST, preferred_element_type=F32
    )


def split3(x):
    high = x.astype(BF16)
    rest = x - high.astype(F32)
    mid = rest.astype(BF16)
    low = (rest - mid.astype(F32)).astype(BF16)
    return high, mid, low


def onehot_dot(x, onehot, dims):
    rows = x.shape[0]
    parts = lax.dot_general(
        jnp.concatenate(split3(x), axis=0),
        onehot,
        (dims, ((), ())),
        preferred_element_type=F32,
    )
    return parts[:rows] + (parts[rows : 2 * rows] + parts[2 * rows :])


def call(kernel, outs, *args, fetched=0, kept=0, placed=0, scratch=(), flops=0):
    vmem = pl.BlockSpec(memory_space=pltpu.VMEM)
    hbm = pl.BlockSpec(memory_space=pltpu.HBM)
    many = isinstance(outs, (list, tuple))
    args = [
        pltpu.with_memory_space_constraint(x, pltpu.HBM) if n < fetched + kept else x
        for n, x in enumerate(args)
    ]
    buffers = [pltpu.VMEM(x.shape, x.dtype) for x in args[:fetched]]

    def wrapped(*refs):
        refs = list(refs)
        extra = refs[len(refs) - fetched - 1 :] if fetched else []
        if fetched:
            refs = refs[: len(refs) - fetched - 1]
            copies = [
                pltpu.make_async_copy(refs[n], extra[n], extra[-1].at[n]) for n in range(fetched)
            ]
            for copy in copies:
                copy.start()
            for copy in copies:
                copy.wait()
            refs[:fetched] = extra[:fetched]
        kernel(*refs)

    scratch = list(scratch)
    if fetched:
        scratch += buffers + [pltpu.SemaphoreType.DMA((fetched,))]
    return pl.pallas_call(
        wrapped,
        out_shape=outs,
        in_specs=[hbm] * (fetched + kept) + [vmem] * (len(args) - fetched - kept),
        out_specs=[hbm] * placed + [vmem] * (len(outs) - placed) if many else vmem,
        scratch_shapes=scratch,
        cost_estimate=pl.CostEstimate(flops=flops, transcendentals=0, bytes_accessed=1 << 20),
        compiler_params=pltpu.CompilerParams(vmem_limit_bytes=8 << 20),
    )(*args)


def shape(*dims):
    return jax.ShapeDtypeStruct(dims, F32)


def pair_scale(rows, diag, off):
    length = rows.shape[1]
    lane = lax.broadcasted_iota(jnp.int32, rows.shape, 1)
    after = pltpu.roll(rows, length - 1, 1)
    before = pltpu.roll(rows, 1, 1)
    return rows * diag + jnp.where(lane % 2 == 0, after, before) * off


def selector_of(perm):
    length = perm.shape[1]
    row = lax.broadcasted_iota(jnp.int32, (length, length), 0)
    return (row == perm).astype(F32).astype(BF16)


def sketch_kernel(
    sketch_ref, perm_ref, kind_ref, values_ref, out_ref, coef_ref, selector_ref
):
    pairs = kind_ref.shape[1]
    length = perm_ref.shape[1]
    one, two, cross = values_ref[0:1, :], values_ref[1:2, :], values_ref[2:3, :]
    twin = kind_ref[...] == 1
    det = one * two - cross * cross
    first = jnp.where(twin, two / det, 1.0 / one)
    second = jnp.where(twin, one / det, 1.0 / two)
    mixed = jnp.where(twin, -cross / det, 0.0)
    row = lax.broadcasted_iota(jnp.int32, (16, pairs), 0)
    stacked = jnp.where(row == 0, first, jnp.where(row == 1, second, mixed))
    pair = lax.broadcasted_iota(jnp.int32, (pairs, length), 0)
    lane = lax.broadcasted_iota(jnp.int32, (pairs, length), 1)
    even = (lane == 2 * pair).astype(F32).astype(BF16)
    odd = (lane == 2 * pair + 1).astype(F32).astype(BF16)
    at_even = onehot_dot(stacked, even, ((1,), (0,)))
    at_odd = onehot_dot(stacked, odd, ((1,), (0,)))
    diag = at_even[0:1] + at_odd[1:2]
    off = at_even[2:3] + at_odd[2:3]
    coef_ref[0:1, :] = diag
    coef_ref[1:2, :] = off
    scaled = pair_scale(sketch_ref[...], diag, off)
    selector = selector_of(perm_ref[...])
    selector_ref[...] = selector
    placed = onehot_dot(scaled, selector, ((1,), (1,)))
    chips, _, width = out_ref.shape
    for chip in range(chips):
        out_ref[chip] = placed[:, chip * width : (chip + 1) * width]


def stages(size):
    bits = []
    bit = size // 2
    while bit:
        bits.append(bit)
        bit //= 2
    return bits


def codes(bits, start=(0,)):
    order = list(start)
    for bit in bits:
        order = order + [code ^ bit for code in order]
    return order


def stack_kernel(*refs):
    piece_refs, out_ref = refs[:-1], refs[-1]
    at = 0
    for piece_ref in piece_refs:
        out_ref[at : at + piece_ref.shape[0]] = piece_ref[...]
        at += piece_ref.shape[0]


def stack(*pieces):
    total = sum(piece.shape[0] for piece in pieces)
    return call(stack_kernel, shape(total, *pieces[0].shape[1:]), *pieces)


def gather(x, bits, send):
    pieces = [x]
    for bit in bits:
        held = pieces[0] if len(pieces) == 1 else stack(*pieces)
        pieces = [held, send(held, bit)]
    return pieces


def entries(refs, order):
    at = 0
    for ref in refs:
        for t in range(ref.shape[0]):
            yield order[at], ref, t
            at += 1


def lanes(ref, *index):
    low, high = index[-2:]
    lead = index[:-2]
    return jnp.concatenate(
        [ref[(chip, *lead, slice(low, high))] for chip in range(ref.shape[0])], axis=1
    )


def load_kernel(*refs):
    count = (len(refs) - 13) // 2
    packed, sources, (out_ref, cols_ref) = refs[:5], refs[5 : 5 + count], refs[5 + count : 7 + count]
    targets, buffers, sems = refs[7 + count : 7 + 2 * count], refs[7 + 2 * count : -1], refs[-1]
    core = lax.axis_index("col") % 2
    pairs = list(zip(packed, buffers))
    for n, (source, target) in enumerate(zip(sources, targets)):
        pairs.append((source.at[core] if n == 0 else source, target))
    copies = [
        pltpu.make_async_copy(source, target, sems.at[n])
        for n, (source, target) in enumerate(pairs)
    ]
    for copy in copies[5:6] + copies[:5] + copies[6:]:
        copy.start()
    for copy in copies[:5]:
        copy.wait()
    row_basis_ref, row_coeff_ref, pivot_ref, col_basis_ref, col_scaled_ref = buffers
    rank = row_basis_ref.shape[1]
    half = rank // 2
    part = row_basis_ref.shape[2]
    for tile in range(2):
        where = slice(tile * part, (tile + 1) * part)
        out_ref[0, :rank, where] = row_basis_ref[tile]
        out_ref[0, rank : 2 * rank, where] = row_coeff_ref[tile]
        out_ref[0, 2 * rank :, where] = pivot_ref[tile * half : (tile + 1) * half]
    for col in range(col_basis_ref.shape[0]):
        base = 2 * col * rank
        cols_ref[0, base : base + rank] = col_basis_ref[col]
        cols_ref[0, base + rank : base + 2 * rank] = col_scaled_ref[col]
    for copy in copies[5:]:
        copy.wait()


def join_kernel(own_ref, other_ref, out_ref):
    core = lax.axis_index("col") % 2
    part = own_ref.shape[0]
    out_ref[pl.ds(pl.multiple_of(core * part, part), part), :] = own_ref[...]
    out_ref[pl.ds(pl.multiple_of((1 - core) * part, part), part), :] = other_ref[core]


def partial_kernel(sketch_ref, own_ref, near_ref, out_ref):
    chip = lax.axis_index("col") // 2
    out_ref[...] = dot_nn(sketch_ref[chip], own_ref[...]) + dot_nn(
        sketch_ref[chip ^ 1], near_ref[...]
    )


def add_kernel(left_ref, right_ref, out_ref):
    out_ref[...] = left_ref[...] + right_ref[...]


def prepare_kernel(order, pivot_ref, *refs):
    count = (len(refs) - 6) // 2
    own_refs, other_refs = refs[:count], refs[count : 2 * count]
    sketch_ref, *panel_refs, factors_ref, corr_ref, updated_ref = refs[2 * count :]
    core = lax.axis_index("col") % 2
    chip = lax.axis_index("col") // 2
    rank = pivot_ref.shape[0]
    part = own_refs[0].shape[2] // 2
    for (code, own_ref, t), (_, other_ref, u) in zip(
        entries(own_refs, order), entries(other_refs, order)
    ):
        mine, theirs = own_ref[t], other_ref[u]
        for tile in range(2):
            where = slice(tile * part, (tile + 1) * part)
            left = jnp.where(core == 0, mine[:, where], theirs[:, where])
            right = jnp.where(core == 0, theirs[:, where], mine[:, where])
            factors_ref[chip ^ code, tile] = jnp.concatenate([left, right], axis=1)
    xrow = lanes(factors_ref, core, 0, rank)
    yrow = lanes(factors_ref, core, rank, 2 * rank)
    pbasis = jnp.concatenate(
        [lanes(factors_ref, tile, 2 * rank, 2 * rank + rank // 2) for tile in range(2)], axis=0
    )
    pcore = dot_nt(yrow, pivot_ref[...])
    mixed = dot_nt(dot_nt(lanes(sketch_ref, 0, rank), pbasis), pcore)
    local = jnp.concatenate(
        [
            jnp.concatenate(
                [
                    factors_ref[chip ^ slot, tile, 2 * rank : 2 * rank + rank // 2, :]
                    for tile in range(2)
                ],
                axis=0,
            )
            for slot in range(len(panel_refs))
        ],
        axis=1,
    )
    sides = jnp.concatenate([mixed, dot_nn(pcore, local).T], axis=0)
    change = dot_nn(sides, xrow)
    corr_ref[...] = change[:rank]
    at = rank
    for slot, panel_ref in enumerate(panel_refs):
        deep = panel_ref.shape[0]
        updated_ref[slot] = panel_ref[...] - change[at : at + deep]
        at += deep


def project_kernel(left_ref, right_ref, corr_ref, updated_ref, range_ref, proj_ref):
    ranges = (left_ref[...] + right_ref[...]) - corr_ref[...]
    range_ref[...] = ranges
    slots, width, _ = updated_ref.shape
    products = dot_nt(
        ranges, jnp.concatenate([updated_ref[slot] for slot in range(slots)], axis=0)
    )
    for slot in range(slots):
        proj_ref[slot] = products[:, slot * width : (slot + 1) * width]


def factor_kernel(
    range_ref, trail_ref, left_ref, right_ref, out_ref, trail_out_ref, held_ref, sems
):
    trail_parts, trail_copies = trail_work(
        trail_ref, left_ref, right_ref, trail_out_ref, held_ref, sems
    )
    rank = range_ref.shape[0]
    gram = dot_nt(range_ref[...], range_ref[...]) / range_ref.shape[1]
    group = 8
    wide = (group, 2 * rank)
    row = lax.broadcasted_iota(jnp.int32, (group, rank), 0)
    col = lax.broadcasted_iota(jnp.int32, (group, rank), 1)
    work = [
        jnp.concatenate(
            [gram[base : base + group], (row + base == col).astype(F32)], axis=1
        )
        for base in range(0, rank, group)
    ]
    rows = lax.broadcasted_iota(jnp.int32, wide, 0)

    def spread(x, lane):
        return jnp.broadcast_to(x[:, lane : lane + 1], wide)

    def pair(top, low, first, cross, second):
        det = first * second - cross * cross
        scale = 1.0 / det
        over = lambda x, y: ((x * second - y * cross) * scale, (y * first - x * cross) * scale)
        root = lax.rsqrt(first)
        done = (top * root, (low - top * (cross / first)) * (lax.rsqrt(det) * (first * root)))
        return over, done

    final = []
    for step in range(0, rank, 4):
        at, inner = divmod(step, group)
        one, two, three, four = [
            jnp.broadcast_to(work[at][inner + n : inner + n + 1], wide) for n in range(4)
        ]
        p11, p12, p13, p14 = [spread(one, step + n) for n in range(4)]
        p22, p23, p24 = [spread(two, step + n) for n in range(1, 4)]
        p33, p34, p44 = spread(three, step + 2), spread(three, step + 3), spread(four, step + 3)
        over, done = pair(one, two, p11, p12, p22)
        u1, u2 = over(one, two)
        u13, u23 = over(p13, p23)
        u14, u24 = over(p14, p24)
        three = three - (p13 * u1 + p23 * u2)
        four = four - (p14 * u1 + p24 * u2)
        over, more = pair(
            three,
            four,
            p33 - (p13 * u13 + p23 * u23),
            p34 - (p13 * u14 + p23 * u24),
            p44 - (p14 * u14 + p24 * u24),
        )
        u3, u4 = over(three, four)
        for index in range(at if inner == 0 else at + 1, len(work)):
            held = work[index]
            h1, h2, h3, h4 = [spread(held, step + n) for n in range(4)]
            h3 = h3 - (h1 * u13 + h2 * u23)
            h4 = h4 - (h1 * u14 + h2 * u24)
            work[index] = held - ((h1 * u1 + h2 * u2) + (h3 * u3 + h4 * u4))
        steps_left = max((rank - step) // 4 - 4, 1)
        for _ in range(-(-len(trail_parts) // steps_left)):
            trail_parts.pop(0)()
        for n, value in enumerate(done + more):
            if inner + n == 0:
                final.append(value)
            else:
                final[at] = jnp.where(rows >= inner + n, value, final[at])
    inverse = jnp.concatenate([block[:, rank:] for block in final], axis=0)
    size = range_ref.shape[1]
    out_ref[:, :size] = dot_nn(inverse, range_ref[...])
    out_ref[:, size : size + rank] = inverse
    for copy in trail_copies:
        copy.wait()


def coeff_of(order, basis_ref, selector_ref, coef_ref, piece_refs, stack_ref):
    chip = lax.axis_index("col") // 2
    rank = basis_ref.shape[0]
    size = selector_ref.shape[1]
    for code, ref, t in entries(piece_refs, order):
        stack_ref[chip ^ code] = ref[t]
    projected = dot_nn(basis_ref[:, size : size + rank], lanes(stack_ref, 0, rank))
    permuted = onehot_dot(projected, selector_ref[...], ((1,), (0,)))
    return pair_scale(permuted, coef_ref[0:1, :], coef_ref[1:2, :]) / jnp.sqrt(jnp.float32(size))


def coeff_kernel(order, basis_ref, selector_ref, coef_ref, *refs):
    out_ref, stack_ref = refs[-2:]
    out_ref[...] = coeff_of(order, basis_ref, selector_ref, coef_ref, refs[:-2], stack_ref)


def finish_kernel(order, basis_ref, own_basis_ref, selector_ref, coef_ref, own_ref, *refs):
    core = lax.axis_index("col") % 2
    basis_out_ref, out_ref, stack_ref, result_ref, sems = refs[-5:]
    size = selector_ref.shape[1]
    copies = [
        pltpu.make_async_copy(source, target, sems.at[n])
        for n, (source, target) in enumerate(
            (
                (own_ref, out_ref.at[core]),
                (own_basis_ref.at[:, :size], basis_out_ref.at[core]),
                (basis_ref.at[:, :size], basis_out_ref.at[1 - core]),
                (result_ref, out_ref.at[1 - core]),
            )
        )
    ]
    for copy in copies[:3]:
        copy.start()
    result_ref[...] = coeff_of(order, basis_ref, selector_ref, coef_ref, refs[:-5], stack_ref)
    copies[3].start()
    for copy in copies:
        copy.wait()


def dot3(left, right, dims):
    high, low = left.astype(BF16), None
    low = (left - high.astype(F32)).astype(BF16)
    top = right.astype(BF16)
    rest = (right - top.astype(F32)).astype(BF16)
    dot = lambda a, b: lax.dot_general(a, b, (dims, ((), ())), preferred_element_type=F32)
    return dot(high, top) + (dot(low, top) + dot(high, rest))


def left_kernel(order, factors_ref, *refs):
    col_refs, (left_ref, right_ref, cols_ref) = refs[:-3], refs[-3:]
    row = lax.axis_index("row")
    tiles, ncols, _, deep = left_ref.shape
    rank = deep // 3
    for code, ref, t in entries(col_refs, order):
        cols_ref[row ^ code] = ref[t]
    for col in range(ncols):
        basis = lanes(cols_ref, 2 * col * rank, (2 * col + 1) * rank)
        high = basis.astype(BF16)
        right_ref[col, :rank, :] = high
        right_ref[col, rank : 2 * rank, :] = high
        right_ref[col, 2 * rank :, :] = (basis - high.astype(F32)).astype(BF16)
    scaled = jnp.concatenate(
        [lanes(cols_ref, (2 * col + 1) * rank, (2 * col + 2) * rank) for col in range(ncols)],
        axis=0,
    )
    yrows = jnp.concatenate(
        [lanes(factors_ref, tile, rank, 2 * rank) for tile in range(tiles)], axis=0
    )
    core = dot3(scaled, yrows, ((1,), (1,)))
    for tile in range(tiles):
        left = dot3(
            core[:, tile * rank : (tile + 1) * rank],
            lanes(factors_ref, tile, 0, rank),
            ((1,), (0,)),
        ).T
        high = left.astype(BF16)
        low = (left - high.astype(F32)).astype(BF16)
        for col in range(ncols):
            part = slice(col * rank, (col + 1) * rank)
            left_ref[tile, col, :, :rank] = high[:, part]
            left_ref[tile, col, :, rank : 2 * rank] = low[:, part]
            left_ref[tile, col, :, 2 * rank :] = high[:, part]


def trail_work(trail_ref, left_ref, right_ref, out_ref, held_ref, sems):
    tiles, ncols, size, _ = left_ref.shape
    groups = right_ref.shape[2] // 128
    step = ncols * groups
    chunks = sems.shape[1]
    rows = size // chunks
    parts, copies = [], []

    def update(tile, chunk, col):
        change = jnp.dot(
            left_ref[tile, col, chunk * rows : (chunk + 1) * rows, :],
            right_ref[col],
            preferred_element_type=F32,
        )
        for group in range(groups):
            where = pl.ds(chunk * rows * step + col * groups + group, rows, stride=step)
            held_ref[tile, where, :] = (
                trail_ref[tile, where, :] - change[:, group * 128 : (group + 1) * 128]
            )
        if col == ncols - 1:
            part = pl.ds(chunk * rows * step, rows * step)
            copy = pltpu.make_async_copy(
                held_ref.at[tile, part], out_ref.at[tile, part], sems.at[tile, chunk]
            )
            copy.start()
            copies.append(copy)

    for tile in range(tiles):
        for chunk in range(chunks):
            for col in range(ncols):
                parts.append(lambda at=(tile, chunk, col): update(*at))
    return parts, copies


def left_call(nrow, order, tiles, size, factors, cols):
    rank = factors.shape[2] * 2 // 5
    ncols = cols[0].shape[1] // (2 * rank)
    return call(
        lambda *refs: left_kernel(order, *refs),
        [
            jax.ShapeDtypeStruct((tiles, ncols, size, 3 * rank), BF16),
            jax.ShapeDtypeStruct((ncols, 3 * rank, nrow * cols[0].shape[2]), BF16),
        ],
        factors,
        *cols,
        scratch=[pltpu.VMEM((nrow, *cols[0].shape[1:]), F32)],
        flops=1 << 26,
    )


def factor_call(ranges, trail, left, right, chunks=4):
    tiles, _, size, ncols, _, width = trail.shape
    rank = ranges.shape[0]
    view = trail.reshape(tiles, size * ncols * width // 128, 128)
    vmem = pl.BlockSpec(memory_space=pltpu.VMEM)
    basis, out = pl.pallas_call(
        factor_kernel,
        out_shape=[shape(rank, ranges.shape[1] + 128), shape(*view.shape)],
        in_specs=[vmem] * 4,
        out_specs=[vmem, pl.BlockSpec(memory_space=pltpu.HBM)],
        scratch_shapes=[
            pltpu.VMEM(view.shape, F32),
            pltpu.SemaphoreType.DMA((tiles, chunks)),
        ],
        cost_estimate=pl.CostEstimate(
            flops=2 * tiles * ncols * size * left.shape[3] * width,
            transcendentals=0,
            bytes_accessed=2 * view.size * 4,
        ),
        compiler_params=pltpu.CompilerParams(vmem_limit_bytes=20 << 20),
        name="factor",
    )(ranges, view, left, right)
    return basis, out.reshape(trail.shape)


def body_of(nrow, ncol):
    chips = ncol // 2
    assert chips > 2 and chips & (chips - 1) == 0 and nrow & (nrow - 1) == 0

    def to_core(x):
        return lax.ppermute(x, "col", [(i, i ^ 1) for i in range(ncol)])

    def to_chip(x, bit):
        return lax.ppermute(x, "col", [(i, i ^ (2 * bit)) for i in range(ncol)])

    def to_row(x, bit):
        return lax.ppermute(x, "row", [(i, i ^ bit) for i in range(nrow)])

    def body(
        trail,
        panel,
        row_basis,
        row_coeff,
        col_basis,
        col_scaled,
        pivot_basis,
        pivot_scaled,
        sketch,
        perm,
        pair_kind,
        pivot_values,
    ):
        _, _, size, part = panel.shape
        rank = sketch.shape[0]
        half = rank // 2
        width = 2 * part
        panel_t = jnp.transpose(panel[:, 0], (0, 2, 1))
        perm_row = perm.reshape(1, -1)
        bits = stages(chips)
        order = codes(bits)
        pair_order = codes(bits[:-1], (0, 1))
        panel_other = to_core(panel_t)
        inputs = (sketch, perm_row, pair_kind.reshape(1, -1), pivot_values, pivot_scaled)
        packed = (row_basis[:, 0], row_coeff[:, 0], pivot_basis, col_basis[:, 0], col_scaled[:, 0])
        factors, columns, panel_own, *loaded, pivot_loaded = call(
            load_kernel,
            [
                shape(1, 2 * rank + half, width),
                shape(1, 2 * rank * col_basis.shape[0], col_basis.shape[3]),
                shape(part, size),
                *[jax.ShapeDtypeStruct(x.shape, x.dtype) for x in inputs],
            ],
            *packed,
            panel_t,
            *inputs,
            kept=6 + len(inputs),
            scratch=[
                *[pltpu.VMEM(x.shape, F32) for x in packed],
                pltpu.SemaphoreType.DMA((6 + len(inputs),)),
            ],
        )
        panel_mine = call(join_kernel, shape(width, size), panel_own, panel_other)
        near = to_chip(panel_mine, 1)
        own = gather(factors, bits, to_chip)
        cols = gather(columns, stages(nrow), to_row)
        sketch_t, coef, selector = call(
            sketch_kernel,
            [shape(chips, rank, width), shape(2, size), jax.ShapeDtypeStruct((size, size), BF16)],
            *loaded,
            flops=1 << 28,
        )
        total = call(partial_kernel, shape(rank, size), sketch_t, panel_mine, near, flops=1 << 26)
        sums = bits[:-1][::-1]
        for bit in sums[:-1]:
            remote = to_chip(total, bit)
            total = call(add_kernel, shape(rank, size), total, remote)
        remote = to_chip(total, sums[-1])
        other = []
        for piece in own:
            other.append(to_core(piece))
        factors_all, corr, updated = call(
            lambda *refs: prepare_kernel(order, *refs),
            [
                shape(chips, 2, 2 * rank + half, width),
                shape(rank, size),
                shape(2, width, size),
            ],
            pivot_loaded,
            *own,
            *other,
            sketch_t,
            panel_mine,
            near,
            flops=1 << 26,
        )
        ranges, proj = call(
            project_kernel,
            [shape(rank, size), shape(2, rank, width)],
            total,
            remote,
            corr,
            updated,
            flops=1 << 26,
        )
        projs = gather(proj, bits[:-1], to_chip)
        left, right = left_call(nrow, codes(stages(nrow)), 2, size, factors_all, cols)
        basis, trail_out = factor_call(ranges, trail, left, right)
        basis_other = to_core(basis)
        projs_other = []
        for piece in projs:
            projs_other.append(to_core(piece))
        scratch = [pltpu.VMEM((chips, rank, width), F32)]
        coeff = call(
            lambda *refs: coeff_kernel(pair_order, *refs),
            shape(rank, size),
            basis,
            selector,
            coef,
            *projs,
            scratch=scratch,
            flops=1 << 28,
        )
        basis_out, coeff_out = call(
            lambda *refs: finish_kernel(pair_order, *refs),
            [shape(2, rank, size)] * 2,
            basis_other,
            basis,
            selector,
            coef,
            coeff,
            *projs_other,
            placed=2,
            scratch=[
                *scratch,
                pltpu.VMEM((rank, size), F32),
                pltpu.SemaphoreType.DMA((4,)),
            ],
            flops=1 << 28,
        )
        return (trail_out, basis_out[:, None], coeff_out[:, None])

    return body


def solution(mesh):
    step = body_of(mesh.shape["row"], mesh.shape["col"])

    return jax.shard_map(
        step,
        mesh=mesh,
        in_specs=(
            P(None, "row", None, None, "col", None),
            P(None, "row", None, "col"),
            P(None, "row", None, "col"),
            P(None, "row", None, "col"),
            P(None, "col", None, "row"),
            P(None, "col", None, "row"),
            P(None, "col"),
            P(),
            P(),
            P(),
            P(),
            P(),
        ),
        out_specs=(
            P(None, "row", None, None, "col", None),
            P(None, "row", None, None),
            P(None, "row", None, None),
        ),
        check_vma=False,
    )
```

```python
import jax
import jax.numpy as jnp
from jax import lax
from jax.experimental import pallas as pl
from jax.experimental.pallas import tpu as pltpu
from jax.sharding import PartitionSpec as P


F32 = jnp.float32
BF16 = jnp.bfloat16
HIGHEST = lax.Precision.HIGHEST
NN = ((1,), (0,))
NT = ((1,), (1,))


def dot_nn(left, right):
    return lax.dot_general(
        left, right, (((1,), (0,)), ((), ())), precision=HIGHEST, preferred_element_type=F32
    )


def dot_nt(left, right):
    return lax.dot_general(
        left, right, (((1,), (1,)), ((), ())), precision=HIGHEST, preferred_element_type=F32
    )


def dot3(left, right, dims):
    high = left.astype(BF16)
    low = (left - high.astype(F32)).astype(BF16)
    top = right.astype(BF16)
    rest = (right - top.astype(F32)).astype(BF16)
    dot = lambda a, b: lax.dot_general(a, b, (dims, ((), ())), preferred_element_type=F32)
    return dot(high, top) + (dot(low, top) + dot(high, rest))


def left_kernel(order, factors_ref, *refs):
    col_refs, (left_ref, right_ref, cols_ref) = refs[:-3], refs[-3:]
    row = lax.axis_index("row")
    tiles, ncols, _, deep = left_ref.shape
    rank = deep // 3
    for code, ref, t in entries(col_refs, order):
        cols_ref[row ^ code] = ref[t]
    for col in range(ncols):
        basis = lanes(cols_ref, 2 * col * rank, (2 * col + 1) * rank)
        high = basis.astype(BF16)
        right_ref[col, :rank, :] = high
        right_ref[col, rank : 2 * rank, :] = high
        right_ref[col, 2 * rank :, :] = (basis - high.astype(F32)).astype(BF16)
    scaled = jnp.concatenate(
        [lanes(cols_ref, (2 * col + 1) * rank, (2 * col + 2) * rank) for col in range(ncols)],
        axis=0,
    )
    yrows = jnp.concatenate(
        [lanes(factors_ref, tile, rank, 2 * rank) for tile in range(tiles)], axis=0
    )
    core = dot3(scaled, yrows, ((1,), (1,)))
    for tile in range(tiles):
        left = dot3(
            core[:, tile * rank : (tile + 1) * rank],
            lanes(factors_ref, tile, 0, rank),
            ((1,), (0,)),
        ).T
        high = left.astype(BF16)
        low = (left - high.astype(F32)).astype(BF16)
        for col in range(ncols):
            part = slice(col * rank, (col + 1) * rank)
            left_ref[tile, col, :, :rank] = high[:, part]
            left_ref[tile, col, :, rank : 2 * rank] = low[:, part]
            left_ref[tile, col, :, 2 * rank :] = high[:, part]


def split3(x):
    high = x.astype(BF16)
    rest = x - high.astype(F32)
    mid = rest.astype(BF16)
    low = (rest - mid.astype(F32)).astype(BF16)
    return high, mid, low


def onehot_dot(x, onehot, dims):
    rows = x.shape[0]
    parts = lax.dot_general(
        jnp.concatenate(split3(x), axis=0),
        onehot,
        (dims, ((), ())),
        preferred_element_type=F32,
    )
    return parts[:rows] + (parts[rows : 2 * rows] + parts[2 * rows :])


def call(kernel, outs, *args, fetched=0, kept=0, placed=0, scratch=(), flops=0):
    vmem = pl.BlockSpec(memory_space=pltpu.VMEM)
    hbm = pl.BlockSpec(memory_space=pltpu.HBM)
    many = isinstance(outs, (list, tuple))
    args = [
        pltpu.with_memory_space_constraint(x, pltpu.HBM) if n < fetched + kept else x
        for n, x in enumerate(args)
    ]
    buffers = [pltpu.VMEM(x.shape, x.dtype) for x in args[:fetched]]

    def wrapped(*refs):
        refs = list(refs)
        extra = refs[len(refs) - fetched - 1 :] if fetched else []
        if fetched:
            refs = refs[: len(refs) - fetched - 1]
            copies = [
                pltpu.make_async_copy(refs[n], extra[n], extra[-1].at[n]) for n in range(fetched)
            ]
            for copy in copies:
                copy.start()
            for copy in copies:
                copy.wait()
            refs[:fetched] = extra[:fetched]
        kernel(*refs)

    scratch = list(scratch)
    if fetched:
        scratch += buffers + [pltpu.SemaphoreType.DMA((fetched,))]
    return pl.pallas_call(
        wrapped,
        out_shape=outs,
        in_specs=[hbm] * (fetched + kept) + [vmem] * (len(args) - fetched - kept),
        out_specs=[hbm] * placed + [vmem] * (len(outs) - placed) if many else vmem,
        scratch_shapes=scratch,
        cost_estimate=pl.CostEstimate(flops=flops, transcendentals=0, bytes_accessed=1 << 20),
        compiler_params=pltpu.CompilerParams(vmem_limit_bytes=8 << 20),
    )(*args)


def shape(*dims):
    return jax.ShapeDtypeStruct(dims, F32)


def pair_scale(rows, diag, off):
    length = rows.shape[1]
    lane = lax.broadcasted_iota(jnp.int32, rows.shape, 1)
    after = pltpu.roll(rows, length - 1, 1)
    before = pltpu.roll(rows, 1, 1)
    return rows * diag + jnp.where(lane % 2 == 0, after, before) * off


def selector_of(perm):
    length = perm.shape[1]
    row = lax.broadcasted_iota(jnp.int32, (length, length), 0)
    return (row == perm).astype(F32).astype(BF16)


def sketch_kernel(
    sketch_ref, perm_ref, kind_ref, values_ref, out_ref, coef_ref, selector_ref
):
    pairs = kind_ref.shape[1]
    length = perm_ref.shape[1]
    one, two, cross = values_ref[0:1, :], values_ref[1:2, :], values_ref[2:3, :]
    twin = kind_ref[...] == 1
    det = one * two - cross * cross
    first = jnp.where(twin, two / det, 1.0 / one)
    second = jnp.where(twin, one / det, 1.0 / two)
    mixed = jnp.where(twin, -cross / det, 0.0)
    row = lax.broadcasted_iota(jnp.int32, (16, pairs), 0)
    stacked = jnp.where(row == 0, first, jnp.where(row == 1, second, mixed))
    pair = lax.broadcasted_iota(jnp.int32, (pairs, length), 0)
    lane = lax.broadcasted_iota(jnp.int32, (pairs, length), 1)
    even = (lane == 2 * pair).astype(F32).astype(BF16)
    odd = (lane == 2 * pair + 1).astype(F32).astype(BF16)
    at_even = onehot_dot(stacked, even, ((1,), (0,)))
    at_odd = onehot_dot(stacked, odd, ((1,), (0,)))
    diag = at_even[0:1] + at_odd[1:2]
    off = at_even[2:3] + at_odd[2:3]
    coef_ref[0:1, :] = diag
    coef_ref[1:2, :] = off
    scaled = pair_scale(sketch_ref[...], diag, off)
    selector = selector_of(perm_ref[...])
    selector_ref[...] = selector
    placed = onehot_dot(scaled, selector, ((1,), (1,)))
    chips, _, width = out_ref.shape
    for chip in range(chips):
        out_ref[chip] = placed[:, chip * width : (chip + 1) * width]


def stages(size):
    bits = []
    bit = size // 2
    while bit:
        bits.append(bit)
        bit //= 2
    return bits


def codes(bits, start=(0,)):
    order = list(start)
    for bit in bits:
        order = order + [code ^ bit for code in order]
    return order


def stack_kernel(*refs):
    piece_refs, out_ref = refs[:-1], refs[-1]
    at = 0
    for piece_ref in piece_refs:
        out_ref[at : at + piece_ref.shape[0]] = piece_ref[...]
        at += piece_ref.shape[0]


def stack(*pieces):
    total = sum(piece.shape[0] for piece in pieces)
    return call(stack_kernel, shape(total, *pieces[0].shape[1:]), *pieces)


def gather(x, bits, send):
    pieces = [x]
    for bit in bits:
        held = pieces[0] if len(pieces) == 1 else stack(*pieces)
        pieces = [held, send(held, bit)]
    return pieces


def entries(refs, order):
    at = 0
    for ref in refs:
        for t in range(ref.shape[0]):
            yield order[at], ref, t
            at += 1


def lanes(ref, *index):
    low, high = index[-2:]
    lead = index[:-2]
    return jnp.concatenate(
        [ref[(chip, *lead, slice(low, high))] for chip in range(ref.shape[0])], axis=1
    )


def load_kernel(*refs):
    count = (len(refs) - 13) // 2
    packed, sources, (out_ref, cols_ref) = refs[:5], refs[5 : 5 + count], refs[5 + count : 7 + count]
    targets, buffers, sems = refs[7 + count : 7 + 2 * count], refs[7 + 2 * count : -1], refs[-1]
    core = lax.axis_index("col") % 2
    pairs = list(zip(packed, buffers))
    for n, (source, target) in enumerate(zip(sources, targets)):
        pairs.append((source.at[core] if n == 0 else source, target))
    copies = [
        pltpu.make_async_copy(source, target, sems.at[n])
        for n, (source, target) in enumerate(pairs)
    ]
    for copy in copies[5:6] + copies[:5] + copies[6:]:
        copy.start()
    for copy in copies[:5]:
        copy.wait()
    row_basis_ref, row_coeff_ref, pivot_ref, col_basis_ref, col_scaled_ref = buffers
    rank = row_basis_ref.shape[1]
    half = rank // 2
    part = row_basis_ref.shape[2]
    for tile in range(2):
        where = slice(tile * part, (tile + 1) * part)
        out_ref[0, :rank, where] = row_basis_ref[tile]
        out_ref[0, rank : 2 * rank, where] = row_coeff_ref[tile]
        out_ref[0, 2 * rank :, where] = pivot_ref[tile * half : (tile + 1) * half]
    for col in range(col_basis_ref.shape[0]):
        base = 2 * col * rank
        cols_ref[0, base : base + rank] = col_basis_ref[col]
        cols_ref[0, base + rank : base + 2 * rank] = col_scaled_ref[col]
    for copy in copies[5:]:
        copy.wait()


def join_kernel(own_ref, other_ref, out_ref):
    core = lax.axis_index("col") % 2
    part = own_ref.shape[0]
    out_ref[pl.ds(pl.multiple_of(core * part, part), part), :] = own_ref[...]
    out_ref[pl.ds(pl.multiple_of((1 - core) * part, part), part), :] = other_ref[core]


def partial_kernel(sketch_ref, own_ref, near_ref, out_ref):
    chip = lax.axis_index("col") // 2
    out_ref[...] = dot_nn(sketch_ref[chip], own_ref[...]) + dot_nn(
        sketch_ref[chip ^ 1], near_ref[...]
    )


def add_kernel(left_ref, right_ref, out_ref):
    out_ref[...] = left_ref[...] + right_ref[...]


def prepare_kernel(order, pivot_ref, *refs):
    count = (len(refs) - 6) // 2
    own_refs, other_refs = refs[:count], refs[count : 2 * count]
    sketch_ref, *panel_refs, factors_ref, corr_ref, updated_ref = refs[2 * count :]
    core = lax.axis_index("col") % 2
    chip = lax.axis_index("col") // 2
    rank = pivot_ref.shape[0]
    part = own_refs[0].shape[2] // 2
    for (code, own_ref, t), (_, other_ref, u) in zip(
        entries(own_refs, order), entries(other_refs, order)
    ):
        mine, theirs = own_ref[t], other_ref[u]
        for tile in range(2):
            where = slice(tile * part, (tile + 1) * part)
            left = jnp.where(core == 0, mine[:, where], theirs[:, where])
            right = jnp.where(core == 0, theirs[:, where], mine[:, where])
            factors_ref[chip ^ code, tile] = jnp.concatenate([left, right], axis=1)
    xrow = lanes(factors_ref, core, 0, rank)
    yrow = lanes(factors_ref, core, rank, 2 * rank)
    pbasis = jnp.concatenate(
        [lanes(factors_ref, tile, 2 * rank, 2 * rank + rank // 2) for tile in range(2)], axis=0
    )
    pcore = dot3(yrow, pivot_ref[...], NT)
    mixed = dot3(dot3(lanes(sketch_ref, 0, rank), pbasis, NT), pcore, NT)
    local = jnp.concatenate(
        [
            jnp.concatenate(
                [
                    factors_ref[chip ^ slot, tile, 2 * rank : 2 * rank + rank // 2, :]
                    for tile in range(2)
                ],
                axis=0,
            )
            for slot in range(len(panel_refs))
        ],
        axis=1,
    )
    sides = jnp.concatenate([mixed, dot3(pcore, local, NN).T], axis=0)
    change = dot3(sides, xrow, NN)
    corr_ref[...] = change[:rank]
    at = rank
    for slot, panel_ref in enumerate(panel_refs):
        deep = panel_ref.shape[0]
        updated_ref[slot] = panel_ref[...] - change[at : at + deep]
        at += deep


def project_kernel(left_ref, right_ref, corr_ref, updated_ref, range_ref, proj_ref):
    ranges = (left_ref[...] + right_ref[...]) - corr_ref[...]
    range_ref[...] = ranges
    slots, width, _ = updated_ref.shape
    products = dot_nt(
        ranges, jnp.concatenate([updated_ref[slot] for slot in range(slots)], axis=0)
    )
    for slot in range(slots):
        proj_ref[slot] = products[:, slot * width : (slot + 1) * width]


def factor_kernel(
    range_ref, trail_ref, left_ref, right_ref, out_ref, trail_out_ref, held_ref, sems
):
    trail_parts, trail_copies = trail_work(
        trail_ref, left_ref, right_ref, trail_out_ref, held_ref, sems
    )
    rank = range_ref.shape[0]
    gram = dot_nt(range_ref[...], range_ref[...]) / range_ref.shape[1]
    group = 8
    wide = (group, 2 * rank)
    row = lax.broadcasted_iota(jnp.int32, (group, rank), 0)
    col = lax.broadcasted_iota(jnp.int32, (group, rank), 1)
    work = [
        jnp.concatenate(
            [gram[base : base + group], (row + base == col).astype(F32)], axis=1
        )
        for base in range(0, rank, group)
    ]
    rows = lax.broadcasted_iota(jnp.int32, wide, 0)

    def spread(x, lane):
        return jnp.broadcast_to(x[:, lane : lane + 1], wide)

    def pair(top, low, first, cross, second):
        det = first * second - cross * cross
        scale = 1.0 / det
        over = lambda x, y: ((x * second - y * cross) * scale, (y * first - x * cross) * scale)
        root = lax.rsqrt(first)
        done = (top * root, (low - top * (cross / first)) * (lax.rsqrt(det) * (first * root)))
        return over, done

    final = []
    for step in range(0, rank, 4):
        at, inner = divmod(step, group)
        one, two, three, four = [
            jnp.broadcast_to(work[at][inner + n : inner + n + 1], wide) for n in range(4)
        ]
        p11, p12, p13, p14 = [spread(one, step + n) for n in range(4)]
        p22, p23, p24 = [spread(two, step + n) for n in range(1, 4)]
        p33, p34, p44 = spread(three, step + 2), spread(three, step + 3), spread(four, step + 3)
        over, done = pair(one, two, p11, p12, p22)
        u1, u2 = over(one, two)
        u13, u23 = over(p13, p23)
        u14, u24 = over(p14, p24)
        three = three - (p13 * u1 + p23 * u2)
        four = four - (p14 * u1 + p24 * u2)
        over, more = pair(
            three,
            four,
            p33 - (p13 * u13 + p23 * u23),
            p34 - (p13 * u14 + p23 * u24),
            p44 - (p14 * u14 + p24 * u24),
        )
        u3, u4 = over(three, four)
        for index in range(at if inner == 0 else at + 1, len(work)):
            held = work[index]
            h1, h2, h3, h4 = [spread(held, step + n) for n in range(4)]
            h3 = h3 - (h1 * u13 + h2 * u23)
            h4 = h4 - (h1 * u14 + h2 * u24)
            work[index] = held - ((h1 * u1 + h2 * u2) + (h3 * u3 + h4 * u4))
        steps_left = max((rank - step) // 4 - 4, 1)
        for _ in range(-(-len(trail_parts) // steps_left)):
            trail_parts.pop(0)()
        for n, value in enumerate(done + more):
            if inner + n == 0:
                final.append(value)
            else:
                final[at] = jnp.where(rows >= inner + n, value, final[at])
    inverse = jnp.concatenate([block[:, rank:] for block in final], axis=0)
    size = range_ref.shape[1]
    out_ref[:, :size] = dot_nn(inverse, range_ref[...])
    out_ref[:, size : size + rank] = inverse
    for copy in trail_copies:
        copy.wait()


def coeff_of(order, basis_ref, selector_ref, coef_ref, piece_refs, stack_ref):
    chip = lax.axis_index("col") // 2
    rank = basis_ref.shape[0]
    size = selector_ref.shape[1]
    for code, ref, t in entries(piece_refs, order):
        stack_ref[chip ^ code] = ref[t]
    projected = dot_nn(basis_ref[:, size : size + rank], lanes(stack_ref, 0, rank))
    permuted = onehot_dot(projected, selector_ref[...], ((1,), (0,)))
    return pair_scale(permuted, coef_ref[0:1, :], coef_ref[1:2, :]) / jnp.sqrt(jnp.float32(size))


def coeff_kernel(order, basis_ref, selector_ref, coef_ref, *refs):
    out_ref, stack_ref = refs[-2:]
    out_ref[...] = coeff_of(order, basis_ref, selector_ref, coef_ref, refs[:-2], stack_ref)


def finish_kernel(order, basis_ref, own_basis_ref, selector_ref, coef_ref, own_ref, *refs):
    core = lax.axis_index("col") % 2
    basis_out_ref, out_ref, stack_ref, result_ref, sems = refs[-5:]
    size = selector_ref.shape[1]
    copies = [
        pltpu.make_async_copy(source, target, sems.at[n])
        for n, (source, target) in enumerate(
            (
                (own_ref, out_ref.at[core]),
                (own_basis_ref.at[:, :size], basis_out_ref.at[core]),
                (basis_ref.at[:, :size], basis_out_ref.at[1 - core]),
                (result_ref, out_ref.at[1 - core]),
            )
        )
    ]
    for copy in copies[:3]:
        copy.start()
    result_ref[...] = coeff_of(order, basis_ref, selector_ref, coef_ref, refs[:-5], stack_ref)
    copies[3].start()
    for copy in copies:
        copy.wait()


def trail_work(trail_ref, left_ref, right_ref, out_ref, held_ref, sems):
    tiles, ncols, size, _ = left_ref.shape
    groups = right_ref.shape[2] // 128
    step = ncols * groups
    chunks = sems.shape[1]
    rows = size // chunks
    parts, copies = [], []

    def update(tile, chunk, col):
        change = jnp.dot(
            left_ref[tile, col, chunk * rows : (chunk + 1) * rows, :],
            right_ref[col],
            preferred_element_type=F32,
        )
        for group in range(groups):
            where = pl.ds(chunk * rows * step + col * groups + group, rows, stride=step)
            held_ref[tile, where, :] = (
                trail_ref[tile, where, :] - change[:, group * 128 : (group + 1) * 128]
            )
        if col == ncols - 1:
            part = pl.ds(chunk * rows * step, rows * step)
            copy = pltpu.make_async_copy(
                held_ref.at[tile, part], out_ref.at[tile, part], sems.at[tile, chunk]
            )
            copy.start()
            copies.append(copy)

    for tile in range(tiles):
        for chunk in range(chunks):
            for col in range(ncols):
                parts.append(lambda at=(tile, chunk, col): update(*at))
    return parts, copies


def left_call(nrow, order, tiles, size, factors, cols):
    rank = factors.shape[2] * 2 // 5
    ncols = cols[0].shape[1] // (2 * rank)
    return call(
        lambda *refs: left_kernel(order, *refs),
        [
            jax.ShapeDtypeStruct((tiles, ncols, size, 3 * rank), BF16),
            jax.ShapeDtypeStruct((ncols, 3 * rank, nrow * cols[0].shape[2]), BF16),
        ],
        factors,
        *cols,
        scratch=[pltpu.VMEM((nrow, *cols[0].shape[1:]), F32)],
        flops=1 << 26,
    )


def factor_call(ranges, trail, left, right, chunks=4):
    tiles, _, size, ncols, _, width = trail.shape
    rank = ranges.shape[0]
    view = trail.reshape(tiles, size * ncols * width // 128, 128)
    vmem = pl.BlockSpec(memory_space=pltpu.VMEM)
    basis, out = pl.pallas_call(
        factor_kernel,
        out_shape=[shape(rank, ranges.shape[1] + 128), shape(*view.shape)],
        in_specs=[vmem] * 4,
        out_specs=[vmem, pl.BlockSpec(memory_space=pltpu.HBM)],
        scratch_shapes=[
            pltpu.VMEM(view.shape, F32),
            pltpu.SemaphoreType.DMA((tiles, chunks)),
        ],
        cost_estimate=pl.CostEstimate(
            flops=2 * tiles * ncols * size * left.shape[3] * width,
            transcendentals=0,
            bytes_accessed=2 * view.size * 4,
        ),
        compiler_params=pltpu.CompilerParams(vmem_limit_bytes=20 << 20),
        name="factor",
    )(ranges, view, left, right)
    return basis, out.reshape(trail.shape)


def body_of(nrow, ncol):
    chips = ncol // 2
    assert chips > 2 and chips & (chips - 1) == 0 and nrow & (nrow - 1) == 0

    def to_core(x):
        return lax.ppermute(x, "col", [(i, i ^ 1) for i in range(ncol)])

    def to_chip(x, bit):
        return lax.ppermute(x, "col", [(i, i ^ (2 * bit)) for i in range(ncol)])

    def to_row(x, bit):
        return lax.ppermute(x, "row", [(i, i ^ bit) for i in range(nrow)])

    def body(
        trail,
        panel,
        row_basis,
        row_coeff,
        col_basis,
        col_scaled,
        pivot_basis,
        pivot_scaled,
        sketch,
        perm,
        pair_kind,
        pivot_values,
    ):
        _, _, size, part = panel.shape
        rank = sketch.shape[0]
        half = rank // 2
        width = 2 * part
        panel_t = jnp.transpose(panel[:, 0], (0, 2, 1))
        perm_row = perm.reshape(1, -1)
        bits = stages(chips)
        order = codes(bits)
        pair_order = codes(bits[:-1], (0, 1))
        panel_other = to_core(panel_t)
        inputs = (sketch, perm_row, pair_kind.reshape(1, -1), pivot_values, pivot_scaled)
        packed = (row_basis[:, 0], row_coeff[:, 0], pivot_basis, col_basis[:, 0], col_scaled[:, 0])
        factors, columns, panel_own, *loaded, pivot_loaded = call(
            load_kernel,
            [
                shape(1, 2 * rank + half, width),
                shape(1, 2 * rank * col_basis.shape[0], col_basis.shape[3]),
                shape(part, size),
                *[jax.ShapeDtypeStruct(x.shape, x.dtype) for x in inputs],
            ],
            *packed,
            panel_t,
            *inputs,
            kept=6 + len(inputs),
            scratch=[
                *[pltpu.VMEM(x.shape, F32) for x in packed],
                pltpu.SemaphoreType.DMA((6 + len(inputs),)),
            ],
        )
        panel_mine = call(join_kernel, shape(width, size), panel_own, panel_other)
        near = to_chip(panel_mine, 1)
        own = gather(factors, bits, to_chip)
        cols = gather(columns, stages(nrow), to_row)
        sketch_t, coef, selector = call(
            sketch_kernel,
            [shape(chips, rank, width), shape(2, size), jax.ShapeDtypeStruct((size, size), BF16)],
            *loaded,
            flops=1 << 28,
        )
        total = call(partial_kernel, shape(rank, size), sketch_t, panel_mine, near, flops=1 << 26)
        sums = bits[:-1][::-1]
        for bit in sums[:-1]:
            remote = to_chip(total, bit)
            total = call(add_kernel, shape(rank, size), total, remote)
        remote = to_chip(total, sums[-1])
        other = []
        for piece in own:
            other.append(to_core(piece))
        factors_all, corr, updated = call(
            lambda *refs: prepare_kernel(order, *refs),
            [
                shape(chips, 2, 2 * rank + half, width),
                shape(rank, size),
                shape(2, width, size),
            ],
            pivot_loaded,
            *own,
            *other,
            sketch_t,
            panel_mine,
            near,
            flops=1 << 26,
        )
        ranges, proj = call(
            project_kernel,
            [shape(rank, size), shape(2, rank, width)],
            total,
            remote,
            corr,
            updated,
            flops=1 << 26,
        )
        projs = gather(proj, bits[:-1], to_chip)
        left, right = left_call(nrow, codes(stages(nrow)), 2, size, factors_all, cols)
        basis, trail_out = factor_call(ranges, trail, left, right)
        basis_other = to_core(basis)
        projs_other = []
        for piece in projs:
            projs_other.append(to_core(piece))
        scratch = [pltpu.VMEM((chips, rank, width), F32)]
        coeff = call(
            lambda *refs: coeff_kernel(pair_order, *refs),
            shape(rank, size),
            basis,
            selector,
            coef,
            *projs,
            scratch=scratch,
            flops=1 << 28,
        )
        basis_out, coeff_out = call(
            lambda *refs: finish_kernel(pair_order, *refs),
            [shape(2, rank, size)] * 2,
            basis_other,
            basis,
            selector,
            coef,
            coeff,
            *projs_other,
            placed=2,
            scratch=[
                *scratch,
                pltpu.VMEM((rank, size), F32),
                pltpu.SemaphoreType.DMA((4,)),
            ],
            flops=1 << 28,
        )
        return (trail_out, basis_out[:, None], coeff_out[:, None])

    return body


def solution(mesh):
    step = body_of(mesh.shape["row"], mesh.shape["col"])

    return jax.shard_map(
        step,
        mesh=mesh,
        in_specs=(
            P(None, "row", None, None, "col", None),
            P(None, "row", None, "col"),
            P(None, "row", None, "col"),
            P(None, "row", None, "col"),
            P(None, "col", None, "row"),
            P(None, "col", None, "row"),
            P(None, "col"),
            P(),
            P(),
            P(),
            P(),
            P(),
        ),
        out_specs=(
            P(None, "row", None, None, "col", None),
            P(None, "row", None, None),
            P(None, "row", None, None),
        ),
        check_vma=False,
    )
```
